32 devices in a mesh: group: 2 (over y), gx: 4 (over z), gy: 2 (over x), gz: 2 (over core).
Axes of the slice: x: 2, y: 2, z: 4, core: 2. Of those that a mesh axis runs over, the one named last changes fastest.
Arguments:
- tokens: bfloat16 [12, 8192], P('group', 'gx'), parts along dimension 0, may hold values from -40 to 40
- norm_gain: float32 [8192], P('gx'), may hold values from 0.1 to 1.9
- q_weight: bfloat16 [8192, 4096], P('gx', ('gy', 'gz')), may hold values from -0.0625 to 0.0625
- kv_weight: bfloat16 [8192, 512], P('gx'), may hold values from -0.0625 to 0.0625
- out_weight: bfloat16 [4096, 8192], P(('gy', 'gz'), 'gx'), may hold values from -0.09375 to 0.09375
- gate_weight: bfloat16 [8192, 16384], P('gx', ('gy', 'gz')), may hold values from -0.0625 to 0.0625
- up_weight: bfloat16 [8192, 16384], P('gx', ('gy', 'gz')), may hold values from -0.0625 to 0.0625
- down_weight: bfloat16 [16384, 8192], P(('gy', 'gz'), 'gx'), may hold values from -0.046875 to 0.046875
- kv_cache: bfloat16 [12, 2048, 512], P(('group', 'gy'), ('gx', 'gz')), parts along dimension 0, may hold values from -55 to 55
- lengths: int32 [12], P(('group', 'gy')), parts along dimension 0, may hold values from 1026 to 2048, as said below
Outputs:
- mixed: bfloat16 [12, 8192], P('group', 'gx'), parts along dimension 0
- new_kv: bfloat16 [12, 512], P(('group', 'gy')), parts along dimension 0
The draws below stay inside these ranges and needn't reach their ends.
There are 2 independent parts, one for each index of `group`. The reference program is written for one: setup_inputs(seed, part) draws one part's arguments, and reference() takes and returns one part's arrays. A program takes and returns all parts, laid end to end along the dimension named above; an argument that names none is the same for every part. Nothing has to cross between parts.
Inputs may be any that keep to these rules, and one draw needn't show every extreme that they name: The new token of sequence s stands at position lengths[s]; cache positions from lengths[s] on hold no valid token; some sequence has all 2048 positions valid.
All inputs are finite; a program needn't handle non-finite values.
Results may differ from the reference program's by a relative error of at most 0.012.
Values may be sent and summed in bfloat16 or wider, within the bound.
A program may use at most 128 MiB of HBM per device.

```python
import jax
import jax.numpy as jnp
from jax import lax

D = 8192
FF = 16384
HEADS = 16
HEAD_DIM = 256
SEQS = 6
CTX = 2048


def draw_tokens(key, part):
    first_key, second_key = jax.random.split(jax.random.fold_in(key, 11), 2)
    place = jnp.arange(D, dtype=jnp.float32) / D
    rough = jax.random.uniform(second_key, (D,), jnp.float32, 0.5, 1.5)
    noise = jax.random.normal(first_key, (SEQS, D), jnp.float32)
    col_scales = 3.0 ** (place - 0.5) * rough
    values = jnp.clip(noise, -4.0, 4.0) * col_scales[None, :]
    return jnp.clip(values, -40.0, 40.0).astype(jnp.bfloat16)


def draw_lengths(key, part):
    first_key, second_key = jax.random.split(jax.random.fold_in(key, 37), 2)
    drawn = jax.random.randint(first_key, (SEQS,), CTX // 2 + 2, CTX + 1)
    full_row = jax.random.randint(second_key, (), 0, SEQS)
    rows = jnp.arange(SEQS, dtype=jnp.int32)
    return jnp.where(rows == full_row, CTX, drawn).astype(jnp.int32)


def draw_kv_cache(key, part):
    first_key = jax.random.fold_in(jax.random.fold_in(key, 23), 0)
    second_key = jax.random.fold_in(jax.random.fold_in(key, 23), 1)
    fourth_key = jax.random.fold_in(jax.random.fold_in(key, 23), 3)
    fifth_key = jax.random.fold_in(jax.random.fold_in(key, 23), 4)
    keys = 2.5 * jnp.clip(jax.random.normal(first_key, (SEQS, CTX, HEAD_DIM), jnp.float32), -4.0, 4.0)
    values = 1.5 * jnp.clip(jax.random.normal(second_key, (SEQS, CTX, HEAD_DIM), jnp.float32), -4.0, 4.0)
    strength = jax.random.uniform(fourth_key, (SEQS, 1, 1), jnp.float32, 30.0, 45.0)
    signs = jax.random.randint(fifth_key, (SEQS, 1, HEAD_DIM), 0, 2).astype(jnp.float32) * 2.0 - 1.0
    factors = jnp.array([1.0, 1.02], jnp.float32)[None, :, None]
    strong = strength * signs * factors
    half = CTX // 2
    keys = jnp.concatenate([keys[:, :half, :], strong, keys[:, half + 2:, :]], 1)
    return jnp.concatenate([keys, values], 2).astype(jnp.bfloat16)


def block_levels(key, dims, cuts, low, largest):
    level = 1.0
    for position, shards_of in cuts:
        heights = jax.random.uniform(jax.random.fold_in(jax.random.fold_in(key, 6), position), (shards_of,), jnp.float32, low / len(cuts), largest / len(cuts))
        level = level * jnp.repeat(jnp.exp(heights), dims[position] // shards_of).reshape((-1,) + (1,) * (len(dims) - 1 - position))
    return level


def centred(key, extent, scale, most, pieces=(), held_as=jnp.bfloat16):
    values = scale * jax.random.normal(key, extent, jnp.float32)
    if pieces:
        values = values * block_levels(key, extent, pieces, -0.22, 0.18)
    return jnp.clip(values, -most, most).astype(held_as)


def setup_inputs(seed: int = 0, part: int = 0) -> dict:
    streams_of = jax.random.split(jax.random.key(seed), 11)
    part_keys = jax.random.split(jax.random.fold_in(streams_of[10], part), 11)
    tokens = draw_tokens(jax.random.fold_in(jax.random.fold_in(streams_of[10], part), 71), part)
    norm_gain = jnp.clip(1.0 + 0.18 * jax.random.normal(streams_of[1], (D,), jnp.float32), 0.1, 1.9)
    q_weight = centred(streams_of[2], (D, HEADS * HEAD_DIM), D ** -0.5, 0.0625, ((0, 4), (1, 4)))
    kv_weight = centred(streams_of[3], (D, 2 * HEAD_DIM), D ** -0.5, 0.0625, ((0, 4),))
    out_weight = centred(streams_of[4], (HEADS * HEAD_DIM, D), (HEADS * HEAD_DIM) ** -0.5, 0.09375, ((0, 4), (1, 4)))
    gate_weight = centred(streams_of[5], (D, FF), D ** -0.5, 0.0625, ((0, 4), (1, 4)))
    up_weight = centred(streams_of[6], (D, FF), D ** -0.5, 0.0625, ((0, 4), (1, 4)))
    down_weight = centred(streams_of[7], (FF, D), FF ** -0.5, 0.046875, ((0, 4), (1, 4)))
    kv_cache = draw_kv_cache(jax.random.fold_in(jax.random.fold_in(streams_of[10], part), 71), part)
    lengths = draw_lengths(jax.random.fold_in(jax.random.fold_in(streams_of[10], part), 71), part)
    return {"tokens": tokens, "norm_gain": norm_gain, "q_weight": q_weight, "kv_weight": kv_weight, "out_weight": out_weight, "gate_weight": gate_weight, "up_weight": up_weight, "down_weight": down_weight, "kv_cache": kv_cache, "lengths": lengths}


epsilon = 1e-05
masked_fill = -1e+30
rotary_base = 10000.0

def rotate(values, angle):
    middle = values.shape[-1] // 2
    first = values[..., :middle]
    second = values[..., middle:]
    cosine = jnp.cos(angle)
    sine_part = jnp.sin(angle)
    return jnp.concatenate([first * cosine - second * sine_part, first * sine_part + second * cosine], -1)

def angles(lengths, head_dim):
    middle = head_dim // 2
    spread = rotary_base ** (-jnp.arange(middle, dtype=jnp.float32) / middle)
    return lengths.astype(jnp.float32)[:, None] * spread[None, :]

def reference(tokens, norm_gain, q_weight, kv_weight, out_weight, gate_weight, up_weight, down_weight, kv_cache, lengths):
    inputs = tokens.astype(jnp.float32)
    center = lax.optimization_barrier(jnp.sum(inputs, 1)) / D
    spread_sq = lax.optimization_barrier(jnp.sum(inputs * inputs, 1)) / D - center * center
    normed = ((inputs - center[:, None]) * lax.rsqrt(spread_sq + epsilon)[:, None] * norm_gain[None, :]).astype(jnp.bfloat16)
    query = jnp.dot(normed, q_weight, preferred_element_type=jnp.float32).astype(jnp.bfloat16)
    keyval = jnp.dot(normed, kv_weight, preferred_element_type=jnp.float32)
    gate = jnp.dot(normed, gate_weight, preferred_element_type=jnp.float32)
    upward = jnp.dot(normed, up_weight, preferred_element_type=jnp.float32)
    hidden = (jax.nn.silu(gate) * upward).astype(jnp.bfloat16)
    angle = angles(lengths, HEAD_DIM)
    new_kv = jnp.concatenate([rotate(keyval[:, :HEAD_DIM], angle), keyval[:, HEAD_DIM:]], 1).astype(jnp.bfloat16)
    rotated = rotate(query.astype(jnp.float32).reshape(SEQS, HEADS, HEAD_DIM), angle[:, None, :]).astype(jnp.bfloat16)
    scale = HEAD_DIM ** (-0.5)
    positions = jnp.arange(CTX, dtype=jnp.int32)

    def one_sequence(packed):
        queries, cache, length, key_new, value_new = packed
        scores = jnp.dot(queries, cache[:, :HEAD_DIM].T, preferred_element_type=jnp.float32) * scale
        own_score = jnp.dot(queries, key_new, preferred_element_type=jnp.float32) * scale
        live = positions < length
        hidden_scores = jnp.where(live[None, :], scores, masked_fill)
        top = jnp.maximum(lax.optimization_barrier(jnp.max(hidden_scores, 1)), own_score)
        weights = jnp.where(live[None, :], jnp.exp(hidden_scores - top[:, None]), 0.0)
        numer = jnp.dot(weights.astype(jnp.bfloat16), cache[:, HEAD_DIM:], preferred_element_type=jnp.float32)
        denom = lax.optimization_barrier(jnp.sum(weights, 1))
        own_weight = jnp.exp(own_score - top)
        numer = numer + own_weight[:, None] * value_new.astype(jnp.float32)[None, :]
        denom = denom + own_weight
        return (numer / denom[:, None]).astype(jnp.bfloat16)
    attended = lax.map(one_sequence, (rotated, kv_cache, lengths, new_kv[:, :HEAD_DIM], new_kv[:, HEAD_DIM:]))
    attended = attended.reshape(SEQS, HEADS * HEAD_DIM)
    total = jnp.dot(attended, out_weight, preferred_element_type=jnp.float32) + jnp.dot(hidden, down_weight, preferred_element_type=jnp.float32)
    mixed = (inputs + total).astype(jnp.bfloat16)
    return (mixed, new_kv)
```

```python
import functools
import itertools

import jax
import jax.numpy as jnp
from jax import lax
from jax.experimental import pallas as pl
from jax.experimental.pallas import tpu as pltpu
from jax.sharding import PartitionSpec as P

D = 8192
HEADS = 16
HEAD_DIM = 256


epsilon = 1e-05
masked_fill = -1e30
rotary_base = 10000.0


def joined(part, axis, combine):
    gathered = jax.tree.map(lambda a: lax.all_gather(a, axis), part)

    def take(source):
        return jax.tree.map(lambda a: lax.dynamic_index_in_dim(a, source, 0, False), gathered)

    return lax.fori_loop(
        1, lax.axis_size(axis), lambda source, state: combine(state, take(source)), take(0)
    )


def rotate(values, angle):
    middle = values.shape[-1] // 2
    first = values[..., :middle]
    second = values[..., middle:]
    cosine = jnp.cos(angle)
    sine_part = jnp.sin(angle)
    return jnp.concatenate(
        [first * cosine - second * sine_part, first * sine_part + second * cosine], -1
    )


def angles(lengths, head_dim):
    middle = head_dim // 2
    spread = rotary_base ** (-jnp.arange(middle, dtype=jnp.float32) / middle)
    return lengths.astype(jnp.float32)[:, None] * spread[None, :]


def combine(earlier, later):
    top = jnp.maximum(earlier[0], later[0])
    first_scale = jnp.exp(earlier[0] - top)
    second_scale = jnp.exp(later[0] - top)
    numer = earlier[1] * first_scale[..., None] + later[1] * second_scale[..., None]
    denom = earlier[2] * first_scale + later[2] * second_scale
    return (top, numer, denom)


def body(
    tokens,
    norm_gain,
    q_weight,
    kv_weight,
    out_weight,
    gate_weight,
    up_weight,
    down_weight,
    kv_cache,
    lengths,
):
    inputs = tokens.astype(jnp.float32)
    totals = lax.psum((jnp.sum(inputs, 1), jnp.sum(inputs * inputs, 1)), "gx")
    center = totals[0] / D
    spread_sq = totals[1] / D - center * center
    normed = (
        (inputs - center[:, None]) * lax.rsqrt(spread_sq + epsilon)[:, None] * norm_gain[None, :]
    ).astype(jnp.bfloat16)
    query_part = jnp.dot(normed, q_weight, preferred_element_type=jnp.float32)
    keyval_part = jnp.dot(normed, kv_weight, preferred_element_type=jnp.float32)
    gate_part = jnp.dot(normed, gate_weight, preferred_element_type=jnp.float32)
    up_part = jnp.dot(normed, up_weight, preferred_element_type=jnp.float32)
    query, keyval, gate, upward = lax.psum((query_part, keyval_part, gate_part, up_part), "gx")
    hidden = (jax.nn.silu(gate) * upward).astype(jnp.bfloat16)
    seq_dev = lengths.shape[0]
    row_groups = lax.axis_size("gy")
    block = q_weight.shape[1]
    first_row = lax.axis_index("gy") * seq_dev
    angle = angles(lengths, HEAD_DIM)
    own_keyval = lax.dynamic_slice_in_dim(keyval, first_row, seq_dev, 0)
    new_kv = jnp.concatenate(
        [rotate(own_keyval[:, :HEAD_DIM], angle), own_keyval[:, HEAD_DIM:]], 1
    ).astype(jnp.bfloat16)
    query_bf = query.astype(jnp.bfloat16)
    every_head = lax.all_gather(query_bf, ("gy", "gz"), axis=1, tiled=True)
    own_query = lax.dynamic_slice_in_dim(every_head, first_row, seq_dev, 0)
    rotated = rotate(
        own_query.astype(jnp.float32).reshape(seq_dev, HEADS, HEAD_DIM), angle[:, None, :]
    ).astype(jnp.bfloat16)
    ctx_dev = kv_cache.shape[1]
    offset = lax.axis_index(("gx", "gz")) * ctx_dev
    positions = offset + jnp.arange(ctx_dev, dtype=jnp.int32)
    live = positions[None, :] < lengths[:, None]
    scale = HEAD_DIM ** (-0.5)
    scores = (
        jnp.einsum(
            "shd,scd->shc", rotated, kv_cache[:, :, :HEAD_DIM], preferred_element_type=jnp.float32
        )
        * scale
    )
    key_new = new_kv[:, :HEAD_DIM]
    value_new = new_kv[:, HEAD_DIM:]
    own_score = (
        jnp.einsum("shd,sd->sh", rotated, key_new, preferred_element_type=jnp.float32) * scale
    )
    hidden_scores = jnp.where(live[:, None, :], scores, masked_fill)
    local_top = jnp.maximum(jnp.max(hidden_scores, 2), own_score)
    weights = jnp.where(live[:, None, :], jnp.exp(hidden_scores - local_top[..., None]), 0.0)
    numer = jnp.einsum(
        "shc,scd->shd",
        weights.astype(jnp.bfloat16),
        kv_cache[:, :, HEAD_DIM:],
        preferred_element_type=jnp.float32,
    )
    denom = jnp.sum(weights, 2)
    top, numer, denom = joined((local_top, numer, denom), ("gx", "gz"), combine)
    own_weight = jnp.exp(own_score - top)
    numer = numer + own_weight[..., None] * value_new.astype(jnp.float32)[:, None, :]
    denom = denom + own_weight
    attended = (numer / denom[..., None]).astype(jnp.bfloat16)
    grouped = attended.reshape(seq_dev, row_groups, HEADS * HEAD_DIM // row_groups)
    picked = lax.dynamic_slice_in_dim(grouped, lax.axis_index("gz") * block, block, 2)
    head_block = lax.all_to_all(picked, "gy", split_axis=1, concat_axis=0, tiled=True).reshape(
        seq_dev * row_groups, block
    )
    partial_value = jnp.dot(head_block, out_weight, preferred_element_type=jnp.float32) + jnp.dot(
        hidden, down_weight, preferred_element_type=jnp.float32
    )
    total = lax.psum(partial_value, ("gy", "gz"))
    mixed = (inputs + total).astype(jnp.bfloat16)
    return (mixed, new_kv)


MESH = pl.DeviceIdType.MESH
F32 = jnp.float32
BF16 = jnp.bfloat16


def kernel(
    dims,
    lengths_ref,
    tokens_h,
    gain_h,
    spread_h,
    q_h,
    kv_h,
    cache_h,
    gate_h,
    up_h,
    out_h,
    down_h,
    mixed_ref,
    newkv_ref,
    tokens_v,
    gain_v,
    spread_v,
    q_v,
    kv_v,
    cache_v,
    gate_v,
    up_v,
    out_v,
    down_v,
    load_sem,
    gu_sem,
    down_sem,
    x_v,
    normed_v,
    stat_v,
    qp_v,
    qrs_v,
    kvs_v,
    qsend_v,
    qall_v,
    rot_v,
    newkv_v,
    part_v,
    prs_v,
    att_v,
    attall_v,
    gsend_v,
    grs_v,
    own_v,
    hid_v,
    acc_v,
    fin_v,
    stat_sem,
    q_sem,
    kvx_sem,
    qa_sem,
    p_sem,
    a_sem,
    a_recv,
    g_sem,
    h_sem,
    f_sem,
):
    ngx, ngy, ngz, rows, rp = dims
    gx, gy, gz = lax.axis_index("gx"), lax.axis_index("gy"), lax.axis_index("gz")
    dx = x_v.shape[1]
    qd = q_v.shape[1]
    heads_dev = qd // HEAD_DIM
    own_heads = heads_dev // ngx
    seq_dev = cache_v.shape[0]
    ctx_dev = cache_v.shape[1]
    fb = gate_v.shape[2]
    owners = ngx * ngz
    part_heads = HEADS // owners
    first = gy * seq_dev
    scale = HEAD_DIM ** (-0.5)
    middle = HEAD_DIM // 2

    small = [
        pltpu.make_async_copy(a, b, load_sem.at[i])
        for i, (a, b) in enumerate(
            (
                (tokens_h, tokens_v),
                (gain_h, gain_v),
                (spread_h, spread_v),
                (q_h, q_v),
                (kv_h, kv_v),
                (cache_h, cache_v),
                (out_h, out_v),
            )
        )
    ]

    def gu_copies(step):
        block = lax.rem(gx + 1 + step, ngx)
        columns = pl.ds(pl.multiple_of(block * fb, fb), fb)
        return (
            pltpu.make_async_copy(gate_h.at[:, columns], gate_v.at[step], gu_sem.at[0, step]),
            pltpu.make_async_copy(up_h.at[:, columns], up_v.at[step], gu_sem.at[1, step]),
        )

    def down_copy(step):
        block = lax.rem(gx + step, ngx)
        picked = pl.ds(pl.multiple_of(block * fb, fb), fb)
        return pltpu.make_async_copy(down_h.at[picked], down_v.at[step], down_sem.at[step])

    for copy in small[:6]:
        copy.start()
    for step in range(ngx):
        for copy in gu_copies(step):
            copy.start()
    small[6].start()
    for step in range(ngx):
        down_copy(step).start()

    offsets = [o for o in itertools.product(range(ngx), range(ngy), range(ngz)) if any(o)]

    def shifted(ox, oy, oz):
        return lax.rem(gx + ox, ngx), lax.rem(gy + oy, ngy), lax.rem(gz + oz, ngz)

    def at(px, py, pz):
        return {"gx": px, "gy": py, "gz": pz}

    barrier = pltpu.get_barrier_semaphore()
    for offset in offsets:
        pl.semaphore_signal(barrier, inc=1, device_id=at(*shifted(*offset)), device_id_type=MESH)

    small[0].wait()
    x_v[...] = jnp.zeros_like(x_v)
    x_v[0:rows, :] = tokens_v[...].astype(F32)
    x = x_v[...]
    lane = lax.broadcasted_iota(jnp.int32, (rp, 128), 1)
    stat_v[gx] = jnp.where(
        lane < 64, jnp.sum(x, 1, keepdims=True), jnp.sum(x * x, 1, keepdims=True)
    )
    pl.semaphore_wait(barrier, len(offsets))

    pending = []

    def send(source, target, sends, receives, device):
        copy = pltpu.make_async_remote_copy(
            src_ref=source,
            dst_ref=target,
            send_sem=sends,
            recv_sem=receives,
            device_id=device,
            device_id_type=MESH,
        )
        copy.start()
        pending.append(copy)

    def arrived(slot, receives):
        pltpu.make_async_remote_copy(
            src_ref=slot,
            dst_ref=slot,
            send_sem=receives,
            recv_sem=receives,
            device_id=at(gx, gy, gz),
            device_id_type=MESH,
        ).wait_recv()

    for k in range(1, ngx):
        peer = lax.rem(gx + k, ngx)
        send(stat_v.at[gx], stat_v.at[gx], stat_sem.at[0, peer], stat_sem.at[1, gx], at(peer, gy, gz))
    small[1].wait()
    small[2].wait()

    row = lax.broadcasted_iota(jnp.int32, (rp, middle), 0)
    length = jnp.zeros((rp, middle), jnp.int32)
    for s in range(seq_dev):
        length = jnp.where(row == first + s, lengths_ref[s], length)
    angle = length.astype(F32) * spread_v[...]
    cosine = jnp.cos(angle)
    sine = jnp.sin(angle)

    for k in range(1, ngx):
        peer = lax.rem(gx + k, ngx)
        arrived(stat_v.at[peer], stat_sem.at[1, peer])
    totals = stat_v[0]
    for k in range(1, ngx):
        totals = totals + stat_v[k]
    center = totals[:, 0:1] / D
    spread_sq = totals[:, 64:65] / D - center * center
    normed_v[...] = ((x_v[...] - center) * lax.rsqrt(spread_sq + epsilon) * gain_v[...]).astype(BF16)

    qo = own_heads * HEAD_DIM
    small[3].wait()

    @pl.loop(0, ngx)
    def _(j):
        columns = pl.ds(pl.multiple_of(j * qo, qo), qo)
        qp_v[j] = jnp.dot(normed_v[...], q_v[:, columns], preferred_element_type=F32)

    for k in range(1, ngx):
        peer = lax.rem(gx + k, ngx)
        send(qp_v.at[peer], qrs_v.at[gx], q_sem.at[0, peer], q_sem.at[1, gx], at(peer, gy, gz))
    small[4].wait()
    kvs_v[gx] = jnp.dot(normed_v[...], kv_v[...], preferred_element_type=F32)
    for k in range(1, ngx):
        peer = lax.rem(gx + k, ngx)
        send(kvs_v.at[gx], kvs_v.at[gx], kvx_sem.at[0, peer], kvx_sem.at[1, gx], at(peer, gy, gz))

    tile = min(512, fb)

    def gate_up(step):
        for copy in gu_copies(step):
            copy.wait()

        @pl.loop(0, fb // tile)
        def _(n):
            columns = pl.ds(pl.multiple_of(n * tile, tile), tile)
            g = jnp.dot(normed_v[...], gate_v[step, :, columns], preferred_element_type=F32)
            u = jnp.dot(normed_v[...], up_v[step, :, columns], preferred_element_type=F32)
            both = jnp.concatenate([g, u], 0)
            if step < ngx - 1:
                gsend_v[step, :, columns] = both.astype(BF16)
            else:
                own_v[:, columns] = both

        if step < ngx - 1:
            peer = lax.rem(gx + 1 + step, ngx)
            send(gsend_v.at[step], grs_v.at[gx], g_sem.at[0, peer], g_sem.at[1, gx], at(peer, gy, gz))

    def gather_query():
        total = qp_v[gx]
        for k in range(1, ngx):
            peer = lax.rem(gx + k, ngx)
            arrived(qrs_v.at[peer], q_sem.at[1, peer])
            total = total + qrs_v[peer]
        mine = (gy * ngz + gz) * heads_dev + gx * own_heads
        for h in range(own_heads):
            piece = total[:, h * HEAD_DIM : (h + 1) * HEAD_DIM].astype(BF16)
            qsend_v[h] = piece
            qall_v[mine + h] = piece
        for offset in offsets:
            px, py, pz = shifted(*offset)
            send(
                qsend_v,
                qall_v.at[pl.ds(mine, own_heads)],
                qa_sem.at[0, px, py, pz],
                qa_sem.at[1, gx, gy, gz],
                at(px, py, pz),
            )

    me_owner = gx * ngz + gz

    def attend():
        keyval = kvs_v[gx]
        for k in range(1, ngx):
            peer = lax.rem(gx + k, ngx)
            arrived(kvs_v.at[peer], kvx_sem.at[1, peer])
            keyval = keyval + kvs_v[peer]
        a = keyval[:, :middle]
        b = keyval[:, middle:HEAD_DIM]
        newkv_v[:, :middle] = a * cosine - b * sine
        newkv_v[:, middle:HEAD_DIM] = a * sine + b * cosine
        newkv_v[:, HEAD_DIM:] = keyval[:, HEAD_DIM:]
        picked = newkv_v[0:seq_dev, :]
        for y in range(1, ngy):
            picked = jnp.where(gy == y, newkv_v[y * seq_dev : (y + 1) * seq_dev, :], picked)
        newkv_ref[...] = picked.astype(BF16)
        for offset in offsets:
            px, py, pz = shifted(*offset)
            slot = (py * ngz + pz) * heads_dev + px * own_heads
            arrived(qall_v.at[pl.ds(slot, own_heads)], qa_sem.at[1, px, py, pz])
        q3 = qall_v[...].astype(F32)
        a = q3[:, :, :middle]
        b = q3[:, :, middle:]
        rot_v[:, :, :middle] = (a * cosine - b * sine).astype(BF16).astype(F32)
        rot_v[:, :, middle:] = (a * sine + b * cosine).astype(BF16).astype(F32)
        small[5].wait()
        rotated = rot_v[...].reshape(HEADS * rp, HEAD_DIM).astype(BF16)
        rowid = lax.rem(lax.broadcasted_iota(jnp.int32, (HEADS * rp, ctx_dev), 0), rp)
        position = (gx * ngz + gz) * ctx_dev + lax.broadcasted_iota(
            jnp.int32, (HEADS * rp, ctx_dev), 1
        )
        scores = jnp.full((HEADS * rp, ctx_dev), masked_fill, F32)
        limit = jnp.zeros((HEADS * rp, ctx_dev), jnp.int32)
        for s in range(seq_dev):
            raw = lax.dot_general(
                rotated,
                cache_v[s, :, :HEAD_DIM],
                (((1,), (1,)), ((), ())),
                preferred_element_type=F32,
            )
            limit = jnp.where(rowid == first + s, lengths_ref[s], limit)
            scores = jnp.where(rowid == first + s, raw * scale, scores)
        live = position < limit
        scores = jnp.where(live, scores, masked_fill)
        top = jnp.max(scores, 1, keepdims=True)
        weights = jnp.where(live, jnp.exp(scores - top), 0.0)
        denom = jnp.sum(weights, 1, keepdims=True)
        numer = jnp.zeros((HEADS * rp, HEAD_DIM), F32)
        for s in range(seq_dev):
            numer = numer + jnp.dot(
                jnp.where(rowid == first + s, weights, 0.0).astype(BF16),
                cache_v[s, :, HEAD_DIM:],
                preferred_element_type=F32,
            )
        lanes = lax.broadcasted_iota(jnp.int32, (HEADS * rp, 128), 1)
        part_v[:, :, :HEAD_DIM] = numer.reshape(HEADS, rp, HEAD_DIM)
        part_v[:, :, HEAD_DIM:] = jnp.where(lanes < 64, top, denom).reshape(HEADS, rp, 128)
        for ox, oz in itertools.product(range(ngx), range(ngz)):
            if ox or oz:
                px, py, pz = shifted(ox, 0, oz)
                peer = px * ngz + pz
                send(
                    part_v.at[pl.ds(peer * part_heads, part_heads)],
                    prs_v.at[me_owner],
                    p_sem.at[0, peer],
                    p_sem.at[1, me_owner],
                    at(px, py, pz),
                )

    block = (me_owner * part_heads) // heads_dev
    by, bz = block // ngz, lax.rem(block, ngz)
    local = lax.rem(me_owner, heads_dev // part_heads)

    def combine_parts():
        prs_v[me_owner] = part_v[pl.ds(me_owner * part_heads, part_heads)]
        for ox, oz in itertools.product(range(ngx), range(ngz)):
            if ox or oz:
                px, py, pz = shifted(ox, 0, oz)
                peer = px * ngz + pz
                arrived(prs_v.at[peer], p_sem.at[1, peer])
        rot = rot_v[pl.ds(me_owner * part_heads, part_heads)]
        newkv = newkv_v[...].astype(BF16).astype(F32)
        own = jnp.sum(rot * newkv[:, :HEAD_DIM], 2, keepdims=True) * scale
        tops = [prs_v[o, :, :, HEAD_DIM : HEAD_DIM + 1] for o in range(owners)]
        top = own
        for t in tops:
            top = jnp.maximum(top, t)
        weight = jnp.exp(own - top)
        numer = weight * newkv[:, HEAD_DIM:]
        denom = weight
        for o in range(owners):
            factor = jnp.exp(tops[o] - top)
            numer = numer + factor * prs_v[o, :, :, :HEAD_DIM]
            denom = denom + factor * prs_v[o, :, :, HEAD_DIM + 64 : HEAD_DIM + 65]
        rowid = lax.broadcasted_iota(jnp.int32, (part_heads, rp, HEAD_DIM), 1)
        mine = (rowid >= first) & (rowid < first + seq_dev)
        att_v[...] = jnp.where(mine, numer / denom, 0.0).astype(BF16)
        for k in range(ngx):
            px = lax.rem(gx + k, ngx)
            copy = pltpu.make_async_remote_copy(
                src_ref=att_v,
                dst_ref=attall_v.at[gy, local],
                send_sem=a_sem.at[px],
                recv_sem=a_recv.at[gy, local],
                device_id=at(px, by, bz),
                device_id_type=MESH,
            )
            if k:
                copy.start()
                pending.append(copy)
            else:
                same = (by == gy) & (bz == gz)

                @pl.when(same)
                def _():
                    attall_v[gy, local] = att_v[...]

                @pl.when(jnp.logical_not(same))
                def _(copy=copy):
                    copy.start()
                    copy.wait_send()

    def out_product():
        for sy in range(ngy):
            for sl in range(heads_dev // part_heads):
                owner = (gy * ngz + gz) * (heads_dev // part_heads) + sl
                theirs = (sy == gy) & (owner == me_owner)

                @pl.when(jnp.logical_not(theirs))
                def _(sy=sy, sl=sl):
                    arrived(attall_v.at[sy, sl], a_recv.at[sy, sl])

        pieces = []
        for h in range(heads_dev):
            total = attall_v[0, h // part_heads, h % part_heads].astype(F32)
            for sy in range(1, ngy):
                total = total + attall_v[sy, h // part_heads, h % part_heads].astype(F32)
            pieces.append(total.astype(BF16))
        mixed_heads = jnp.concatenate(pieces, 1)
        small[6].wait()
        ct = min(512, dx)
        normed_v[:, :qd] = mixed_heads

        @pl.loop(0, dx // ct)
        def _(n):
            columns = pl.ds(pl.multiple_of(n * ct, ct), ct)
            acc_v[:, columns] = jnp.dot(
                normed_v[:, :qd], out_v[:, columns], preferred_element_type=F32
            )

    gate_up(0)
    gather_query()
    gate_up(1)
    attend()
    gate_up(2)
    combine_parts()
    for step in range(3, ngx):
        gate_up(step)

    both = own_v[...]
    for k in range(1, ngx):
        peer = lax.rem(gx + k, ngx)
        arrived(grs_v.at[peer], g_sem.at[1, peer])
        both = both + grs_v[peer].astype(F32)
    g = both[:rp]
    u = both[rp:]
    hid_v[gx] = (g / (1.0 + jnp.exp(-g)) * u).astype(BF16)
    for k in range(1, ngx):
        peer = lax.rem(gx + k, ngx)
        send(hid_v.at[gx], hid_v.at[gx], h_sem.at[0, peer], h_sem.at[1, gx], at(peer, gy, gz))

    out_product()
    spot = gy * ngz + gz
    ct = min(512, dx)
    for step in range(ngx):
        source = lax.rem(gx + step, ngx)
        down_copy(step).wait()
        if step:
            arrived(hid_v.at[source], h_sem.at[1, source])

        @pl.loop(0, dx // ct)
        def _(n):
            columns = pl.ds(pl.multiple_of(n * ct, ct), ct)
            acc_v[:, columns] += jnp.dot(
                hid_v[source], down_v[step, :, columns], preferred_element_type=F32
            )

    fin_v[spot] = acc_v[...].astype(BF16)
    peers = [o for o in itertools.product(range(ngy), range(ngz)) if any(o)]
    for oy, oz in peers:
        px, py, pz = shifted(0, oy, oz)
        peer = py * ngz + pz
        send(fin_v.at[spot], fin_v.at[spot], f_sem.at[0, peer], f_sem.at[1, spot], at(px, py, pz))
    total = x_v[...] + acc_v[...]
    for oy, oz in peers:
        px, py, pz = shifted(0, oy, oz)
        peer = py * ngz + pz
        arrived(fin_v.at[peer], f_sem.at[1, peer])
        total = total + fin_v[peer].astype(F32)
    mixed_ref[...] = total[:rows].astype(BF16)
    for copy in pending:
        copy.wait_send()


def fused(sizes, *args):
    (tokens, gain, qw, kvw, outw, gatew, upw, downw, cache, lengths) = args
    ngx, ngy, ngz = sizes
    rows, dx = tokens.shape
    rp = -(-rows // 8) * 8
    qd = qw.shape[1]
    fb = gatew.shape[1] // ngx
    own_heads = qd // HEAD_DIM // ngx
    heads_dev = qd // HEAD_DIM
    owners = ngx * ngz
    part_heads = HEADS // owners
    middle = HEAD_DIM // 2
    spread = (rotary_base ** (-jnp.arange(middle, dtype=F32) / middle)).reshape(1, middle)
    dma = pltpu.SemaphoreType.DMA
    vm = pltpu.VMEM
    scratch = [
        vm(tokens.shape, BF16),
        vm((1, dx), F32),
        vm((1, middle), F32),
        vm(qw.shape, BF16),
        vm(kvw.shape, BF16),
        vm(cache.shape, BF16),
        vm((ngx, dx, fb), BF16),
        vm((ngx, dx, fb), BF16),
        vm(outw.shape, BF16),
        vm((ngx, fb, dx), BF16),
        dma((7,)),
        dma((2, ngx)),
        dma((ngx,)),
        vm((rp, dx), F32),
        vm((rp, dx), BF16),
        vm((ngx, rp, 128), F32),
        vm((ngx, rp, own_heads * HEAD_DIM), F32),
        vm((ngx, rp, own_heads * HEAD_DIM), F32),
        vm((ngx, rp, 2 * HEAD_DIM), F32),
        vm((own_heads, rp, HEAD_DIM), BF16),
        vm((HEADS, rp, HEAD_DIM), BF16),
        vm((HEADS, rp, HEAD_DIM), F32),
        vm((rp, 2 * HEAD_DIM), F32),
        vm((HEADS, rp, HEAD_DIM + 128), F32),
        vm((owners, part_heads, rp, HEAD_DIM + 128), F32),
        vm((part_heads, rp, HEAD_DIM), BF16),
        vm((ngy, heads_dev // part_heads, part_heads, rp, HEAD_DIM), BF16),
        vm((ngx - 1, 2 * rp, fb), BF16),
        vm((ngx, 2 * rp, fb), BF16),
        vm((2 * rp, fb), F32),
        vm((ngx, rp, fb), BF16),
        vm((rp, dx), F32),
        vm((ngy * ngz, rp, dx), BF16),
        dma((2, ngx)),
        dma((2, ngx)),
        dma((2, ngx)),
        dma((2, ngx, ngy, ngz)),
        dma((2, owners)),
        dma((ngx,)),
        dma((ngy, heads_dev // part_heads)),
        dma((2, ngx)),
        dma((2, ngx)),
        dma((2, ngy * ngz)),
    ]
    anywhere = pl.BlockSpec(memory_space=pl.ANY)
    return pl.pallas_call(
        functools.partial(kernel, (ngx, ngy, ngz, rows, rp)),
        out_shape=(
            jax.ShapeDtypeStruct(tokens.shape, BF16),
            jax.ShapeDtypeStruct((cache.shape[0], 2 * HEAD_DIM), BF16),
        ),
        in_specs=[pl.BlockSpec(memory_space=pltpu.SMEM)] + [anywhere] * 10,
        out_specs=(pl.BlockSpec(memory_space=pltpu.VMEM),) * 2,
        scratch_shapes=scratch,
        compiler_params=pltpu.CompilerParams(
            collective_id=0, has_side_effects=True, vmem_limit_bytes=67043328
        ),
    )(lengths, tokens, gain.reshape(1, dx), spread, qw, kvw, cache, gatew, upw, outw, downw)


def fits(sizes, q_dev, ff_dev, weight_bytes):
    ngx, ngy, ngz = sizes
    heads_dev = q_dev // HEAD_DIM
    return (
        ngx >= 3
        and heads_dev % ngx == 0
        and HEADS % (ngx * ngz) == 0
        and heads_dev % (HEADS // (ngx * ngz)) == 0
        and ff_dev % (ngx * 128) == 0
        and weight_bytes <= 60 * 2**20
    )


def choose(sizes, *args):
    held = sum(a.size * a.dtype.itemsize for a in args[2:9])
    if fits(sizes, args[2].shape[1], args[5].shape[1], held):
        return fused(sizes, *args)
    return body(*args)


def solution(mesh):
    sizes = tuple(mesh.shape[a] for a in ("gx", "gy", "gz"))
    chosen = functools.partial(choose, sizes)
    in_specs = (
        P("group", "gx"),
        P("gx"),
        P("gx", ("gy", "gz")),
        P("gx", None),
        P(("gy", "gz"), "gx"),
        P("gx", ("gy", "gz")),
        P("gx", ("gy", "gz")),
        P(("gy", "gz"), "gx"),
        P(("group", "gy"), ("gx", "gz"), None),
        P(("group", "gy")),
    )
    out_specs = (P("group", "gx"), P(("group", "gy"), None))
    return jax.shard_map(chosen, mesh=mesh, in_specs=in_specs, out_specs=out_specs, check_vma=False)
```

```python
import functools
import itertools

import jax
import jax.numpy as jnp
from jax import lax
from jax.experimental import pallas as pl
from jax.experimental.pallas import tpu as pltpu
from jax.sharding import PartitionSpec as P

D = 8192
HEADS = 16
HEAD_DIM = 256


epsilon = 1e-05
masked_fill = -1e30
rotary_base = 10000.0


def joined(part, axis, combine):
    gathered = jax.tree.map(lambda a: lax.all_gather(a, axis), part)

    def take(source):
        return jax.tree.map(lambda a: lax.dynamic_index_in_dim(a, source, 0, False), gathered)

    return lax.fori_loop(
        1, lax.axis_size(axis), lambda source, state: combine(state, take(source)), take(0)
    )


def rotate(values, angle):
    middle = values.shape[-1] // 2
    first = values[..., :middle]
    second = values[..., middle:]
    cosine = jnp.cos(angle)
    sine_part = jnp.sin(angle)
    return jnp.concatenate(
        [first * cosine - second * sine_part, first * sine_part + second * cosine], -1
    )


def angles(lengths, head_dim):
    middle = head_dim // 2
    spread = rotary_base ** (-jnp.arange(middle, dtype=jnp.float32) / middle)
    return lengths.astype(jnp.float32)[:, None] * spread[None, :]


def combine(earlier, later):
    top = jnp.maximum(earlier[0], later[0])
    first_scale = jnp.exp(earlier[0] - top)
    second_scale = jnp.exp(later[0] - top)
    numer = earlier[1] * first_scale[..., None] + later[1] * second_scale[..., None]
    denom = earlier[2] * first_scale + later[2] * second_scale
    return (top, numer, denom)


def body(
    tokens,
    norm_gain,
    q_weight,
    kv_weight,
    out_weight,
    gate_weight,
    up_weight,
    down_weight,
    kv_cache,
    lengths,
):
    inputs = tokens.astype(jnp.float32)
    totals = lax.psum((jnp.sum(inputs, 1), jnp.sum(inputs * inputs, 1)), "gx")
    center = totals[0] / D
    spread_sq = totals[1] / D - center * center
    normed = (
        (inputs - center[:, None]) * lax.rsqrt(spread_sq + epsilon)[:, None] * norm_gain[None, :]
    ).astype(jnp.bfloat16)
    query_part = jnp.dot(normed, q_weight, preferred_element_type=jnp.float32)
    keyval_part = jnp.dot(normed, kv_weight, preferred_element_type=jnp.float32)
    gate_part = jnp.dot(normed, gate_weight, preferred_element_type=jnp.float32)
    up_part = jnp.dot(normed, up_weight, preferred_element_type=jnp.float32)
    query, keyval, gate, upward = lax.psum((query_part, keyval_part, gate_part, up_part), "gx")
    hidden = (jax.nn.silu(gate) * upward).astype(jnp.bfloat16)
    seq_dev = lengths.shape[0]
    row_groups = lax.axis_size("gy")
    block = q_weight.shape[1]
    first_row = lax.axis_index("gy") * seq_dev
    angle = angles(lengths, HEAD_DIM)
    own_keyval = lax.dynamic_slice_in_dim(keyval, first_row, seq_dev, 0)
    new_kv = jnp.concatenate(
        [rotate(own_keyval[:, :HEAD_DIM], angle), own_keyval[:, HEAD_DIM:]], 1
    ).astype(jnp.bfloat16)
    query_bf = query.astype(jnp.bfloat16)
    every_head = lax.all_gather(query_bf, ("gy", "gz"), axis=1, tiled=True)
    own_query = lax.dynamic_slice_in_dim(every_head, first_row, seq_dev, 0)
    rotated = rotate(
        own_query.astype(jnp.float32).reshape(seq_dev, HEADS, HEAD_DIM), angle[:, None, :]
    ).astype(jnp.bfloat16)
    ctx_dev = kv_cache.shape[1]
    offset = lax.axis_index(("gx", "gz")) * ctx_dev
    positions = offset + jnp.arange(ctx_dev, dtype=jnp.int32)
    live = positions[None, :] < lengths[:, None]
    scale = HEAD_DIM ** (-0.5)
    scores = (
        jnp.einsum(
            "shd,scd->shc", rotated, kv_cache[:, :, :HEAD_DIM], preferred_element_type=jnp.float32
        )
        * scale
    )
    key_new = new_kv[:, :HEAD_DIM]
    value_new = new_kv[:, HEAD_DIM:]
    own_score = (
        jnp.einsum("shd,sd->sh", rotated, key_new, preferred_element_type=jnp.float32) * scale
    )
    hidden_scores = jnp.where(live[:, None, :], scores, masked_fill)
    local_top = jnp.maximum(jnp.max(hidden_scores, 2), own_score)
    weights = jnp.where(live[:, None, :], jnp.exp(hidden_scores - local_top[..., None]), 0.0)
    numer = jnp.einsum(
        "shc,scd->shd",
        weights.astype(jnp.bfloat16),
        kv_cache[:, :, HEAD_DIM:],
        preferred_element_type=jnp.float32,
    )
    denom = jnp.sum(weights, 2)
    top, numer, denom = joined((local_top, numer, denom), ("gx", "gz"), combine)
    own_weight = jnp.exp(own_score - top)
    numer = numer + own_weight[..., None] * value_new.astype(jnp.float32)[:, None, :]
    denom = denom + own_weight
    attended = (numer / denom[..., None]).astype(jnp.bfloat16)
    grouped = attended.reshape(seq_dev, row_groups, HEADS * HEAD_DIM // row_groups)
    picked = lax.dynamic_slice_in_dim(grouped, lax.axis_index("gz") * block, block, 2)
    head_block = lax.all_to_all(picked, "gy", split_axis=1, concat_axis=0, tiled=True).reshape(
        seq_dev * row_groups, block
    )
    partial_value = jnp.dot(head_block, out_weight, preferred_element_type=jnp.float32) + jnp.dot(
        hidden, down_weight, preferred_element_type=jnp.float32
    )
    total = lax.psum(partial_value, ("gy", "gz"))
    mixed = (inputs + total).astype(jnp.bfloat16)
    return (mixed, new_kv)


MESH = pl.DeviceIdType.MESH
F32 = jnp.float32
BF16 = jnp.bfloat16


def kernel(
    dims,
    lengths_ref,
    tokens_h,
    gain_h,
    spread_h,
    q_h,
    kv_h,
    cache_h,
    gate_h,
    up_h,
    out_h,
    down_h,
    mixed_ref,
    newkv_ref,
    tokens_v,
    gain_v,
    spread_v,
    q_v,
    kv_v,
    cache_v,
    gate_v,
    up_v,
    out_v,
    down_v,
    load_sem,
    gu_sem,
    down_sem,
    x_v,
    normed_v,
    stat_v,
    qp_v,
    qrs_v,
    kvs_v,
    qsend_v,
    qall_v,
    rot_v,
    newkv_v,
    part_v,
    prs_v,
    side_v,
    srs_v,
    att_v,
    attall_v,
    gsend_v,
    grs_v,
    own_v,
    hid_v,
    acc_v,
    heads_v,
    fin_v,
    stat_sem,
    q_sem,
    kvx_sem,
    qa_sem,
    p_sem,
    s_sem,
    a_sem,
    a_recv,
    g_sem,
    h_sem,
    f_sem,
):
    ngx, ngy, ngz, rows, rp = dims
    gx, gy, gz = lax.axis_index("gx"), lax.axis_index("gy"), lax.axis_index("gz")
    dx = x_v.shape[1]
    qd = q_v.shape[1]
    heads_dev = qd // HEAD_DIM
    own_heads = heads_dev // ngx
    seq_dev = cache_v.shape[0]
    ctx_dev = cache_v.shape[1]
    fb = gate_v.shape[2]
    owners = ngx * ngz
    part_heads = HEADS // owners
    first = gy * seq_dev
    scale = HEAD_DIM ** (-0.5)
    middle = HEAD_DIM // 2

    small = [
        pltpu.make_async_copy(a, b, load_sem.at[i])
        for i, (a, b) in enumerate(
            (
                (tokens_h, tokens_v),
                (gain_h, gain_v),
                (spread_h, spread_v),
                (q_h, q_v),
                (kv_h, kv_v),
                (cache_h, cache_v),
                (out_h, out_v),
            )
        )
    ]

    def gu_copies(step):
        block = lax.rem(gx + 1 + step, ngx)
        columns = pl.ds(pl.multiple_of(block * fb, fb), fb)
        return (
            pltpu.make_async_copy(gate_h.at[:, columns], gate_v.at[step], gu_sem.at[0, step]),
            pltpu.make_async_copy(up_h.at[:, columns], up_v.at[step], gu_sem.at[1, step]),
        )

    def down_copy(step):
        block = lax.rem(gx + step, ngx)
        picked = pl.ds(pl.multiple_of(block * fb, fb), fb)
        return pltpu.make_async_copy(down_h.at[picked], down_v.at[step], down_sem.at[step])

    for copy in small[:6]:
        copy.start()
    for step in range(ngx):
        for copy in gu_copies(step):
            copy.start()
    small[6].start()
    for step in range(ngx):
        down_copy(step).start()

    offsets = [o for o in itertools.product(range(ngx), range(ngy), range(ngz)) if any(o)]

    def shifted(ox, oy, oz):
        return lax.rem(gx + ox, ngx), lax.rem(gy + oy, ngy), lax.rem(gz + oz, ngz)

    def at(px, py, pz):
        return {"gx": px, "gy": py, "gz": pz}

    barrier = pltpu.get_barrier_semaphore()
    for offset in offsets:
        pl.semaphore_signal(barrier, inc=1, device_id=at(*shifted(*offset)), device_id_type=MESH)

    small[0].wait()
    x_v[...] = jnp.zeros_like(x_v)
    x_v[0:rows, :] = tokens_v[...].astype(F32)
    x = x_v[...]
    lane = lax.broadcasted_iota(jnp.int32, (rp, 128), 1)
    stat_v[gx] = jnp.where(
        lane < 64, jnp.sum(x, 1, keepdims=True), jnp.sum(x * x, 1, keepdims=True)
    )
    small[1].wait()
    spare = lax.broadcasted_iota(jnp.int32, (rp, dx), 0) == rows
    local_mean = stat_v[gx][:, 0:1] / dx
    centred = jnp.where(spare, 1.0, x - local_mean)
    normed_v[...] = (centred * gain_v[...]).astype(BF16)

    qo = own_heads * HEAD_DIM
    small[3].wait()

    @pl.loop(0, ngx)
    def _(j):
        columns = pl.ds(pl.multiple_of(j * qo, qo), qo)
        qp_v[j] = jnp.dot(normed_v[...], q_v[:, columns], preferred_element_type=F32)

    pl.semaphore_wait(barrier, len(offsets))

    pending = []

    def send(source, target, sends, receives, device):
        copy = pltpu.make_async_remote_copy(
            src_ref=source,
            dst_ref=target,
            send_sem=sends,
            recv_sem=receives,
            device_id=device,
            device_id_type=MESH,
        )
        copy.start()
        pending.append(copy)

    def arrived(slot, receives):
        pltpu.make_async_remote_copy(
            src_ref=slot,
            dst_ref=slot,
            send_sem=receives,
            recv_sem=receives,
            device_id=at(gx, gy, gz),
            device_id_type=MESH,
        ).wait_recv()

    for k in range(1, ngx):
        peer = lax.rem(gx + k, ngx)
        send(stat_v.at[gx], stat_v.at[gx], stat_sem.at[0, peer], stat_sem.at[1, gx], at(peer, gy, gz))
        send(qp_v.at[peer], qrs_v.at[gx], q_sem.at[0, peer], q_sem.at[1, gx], at(peer, gy, gz))
    small[4].wait()
    kvs_v[gx] = jnp.dot(normed_v[...], kv_v[...], preferred_element_type=F32)
    for k in range(1, ngx):
        peer = lax.rem(gx + k, ngx)
        send(kvs_v.at[gx], kvs_v.at[gx], kvx_sem.at[0, peer], kvx_sem.at[1, gx], at(peer, gy, gz))
    small[2].wait()

    row = lax.broadcasted_iota(jnp.int32, (rp, middle), 0)
    length = jnp.zeros((rp, middle), jnp.int32)
    for s in range(seq_dev):
        length = jnp.where(row == first + s, lengths_ref[s], length)
    angle = length.astype(F32) * spread_v[...]
    cosine = jnp.cos(angle)
    sine = jnp.sin(angle)

    def moments():
        for k in range(1, ngx):
            peer = lax.rem(gx + k, ngx)
            arrived(stat_v.at[peer], stat_sem.at[1, peer])
        totals = stat_v[0]
        for k in range(1, ngx):
            totals = totals + stat_v[k]
        center = totals[:, 0:1] / D
        spread_sq = totals[:, 64:65] / D - center * center
        return center, lax.rsqrt(spread_sq + epsilon)

    def corrected(part, gain_row, source, center):
        return part + (stat_v[source][:, 0:1] / dx - center) * gain_row

    tile = min(512, fb)

    def gate_up(step):
        for copy in gu_copies(step):
            copy.wait()

        @pl.loop(0, fb // tile)
        def _(n):
            columns = pl.ds(pl.multiple_of(n * tile, tile), tile)
            g = jnp.dot(normed_v[...], gate_v[step, :, columns], preferred_element_type=F32)
            u = jnp.dot(normed_v[...], up_v[step, :, columns], preferred_element_type=F32)
            both = jnp.concatenate([g, u], 0)
            if step < ngx - 1:
                gsend_v[step, :, columns] = both.astype(BF16)
            else:
                own_v[:, columns] = both

        if step < ngx - 1:
            peer = lax.rem(gx + 1 + step, ngx)
            send(gsend_v.at[step], grs_v.at[gx], g_sem.at[0, peer], g_sem.at[1, gx], at(peer, gy, gz))

    def gather_query():
        qrs_v[gx] = qp_v[gx]
        total = None
        for k in range(ngx):
            peer = lax.rem(gx + k, ngx)
            if k:
                arrived(qrs_v.at[peer], q_sem.at[1, peer])
            part = corrected(qrs_v[peer], qrs_v[peer, rows : rows + 1, :], peer, center)
            total = part if total is None else total + part
        total = total * inverse
        mine = (gy * ngz + gz) * heads_dev + gx * own_heads
        for h in range(own_heads):
            piece = total[:, h * HEAD_DIM : (h + 1) * HEAD_DIM].astype(BF16)
            qsend_v[h] = piece
            qall_v[mine + h] = piece
        for offset in offsets:
            px, py, pz = shifted(*offset)
            send(
                qsend_v,
                qall_v.at[pl.ds(mine, own_heads)],
                qa_sem.at[0, px, py, pz],
                qa_sem.at[1, gx, gy, gz],
                at(px, py, pz),
            )

    me_owner = gx * ngz + gz

    def attend():
        keyval = None
        for k in range(ngx):
            peer = lax.rem(gx + k, ngx)
            if k:
                arrived(kvs_v.at[peer], kvx_sem.at[1, peer])
            part = corrected(kvs_v[peer], kvs_v[peer, rows : rows + 1, :], peer, center)
            keyval = part if keyval is None else keyval + part
        keyval = keyval * inverse
        a = keyval[:, :middle]
        b = keyval[:, middle:HEAD_DIM]
        newkv_v[:, :middle] = a * cosine - b * sine
        newkv_v[:, middle:HEAD_DIM] = a * sine + b * cosine
        newkv_v[:, HEAD_DIM:] = keyval[:, HEAD_DIM:]
        picked = newkv_v[0:seq_dev, :]
        for y in range(1, ngy):
            picked = jnp.where(gy == y, newkv_v[y * seq_dev : (y + 1) * seq_dev, :], picked)
        newkv_ref[...] = picked.astype(BF16)
        for offset in offsets:
            px, py, pz = shifted(*offset)
            slot = (py * ngz + pz) * heads_dev + px * own_heads
            arrived(qall_v.at[pl.ds(slot, own_heads)], qa_sem.at[1, px, py, pz])
        q3 = qall_v[...].astype(F32)
        a = q3[:, :, :middle]
        b = q3[:, :, middle:]
        rot_v[:, :, :middle] = (a * cosine - b * sine).astype(BF16).astype(F32)
        rot_v[:, :, middle:] = (a * sine + b * cosine).astype(BF16).astype(F32)
        small[5].wait()
        rotated = rot_v[...].reshape(HEADS * rp, HEAD_DIM).astype(BF16)
        rowid = lax.rem(lax.broadcasted_iota(jnp.int32, (HEADS * rp, ctx_dev), 0), rp)
        position = (gx * ngz + gz) * ctx_dev + lax.broadcasted_iota(
            jnp.int32, (HEADS * rp, ctx_dev), 1
        )
        scores = jnp.full((HEADS * rp, ctx_dev), masked_fill, F32)
        limit = jnp.zeros((HEADS * rp, ctx_dev), jnp.int32)
        for s in range(seq_dev):
            raw = lax.dot_general(
                rotated,
                cache_v[s, :, :HEAD_DIM],
                (((1,), (1,)), ((), ())),
                preferred_element_type=F32,
            )
            limit = jnp.where(rowid == first + s, lengths_ref[s], limit)
            scores = jnp.where(rowid == first + s, raw * scale, scores)
        live = position < limit
        scores = jnp.where(live, scores, masked_fill)
        top = jnp.max(scores, 1, keepdims=True)
        weights = jnp.where(live, jnp.exp(scores - top), 0.0)
        denom = jnp.sum(weights, 1, keepdims=True)
        numer = jnp.zeros((HEADS * rp, HEAD_DIM), F32)
        for s in range(seq_dev):
            numer = numer + jnp.dot(
                jnp.where(rowid == first + s, weights, 0.0).astype(BF16),
                cache_v[s, :, HEAD_DIM:],
                preferred_element_type=F32,
            )
        part_v[...] = numer.reshape(HEADS, rp, HEAD_DIM).astype(BF16)
        wide = 64 // part_heads
        lanes = lax.broadcasted_iota(jnp.int32, (owners, rp, 128), 2)
        top4 = jnp.broadcast_to(top, (HEADS * rp, 128)).reshape(owners, part_heads, rp, 128)
        denom4 = jnp.broadcast_to(denom, (HEADS * rp, 128)).reshape(owners, part_heads, rp, 128)
        packed = jnp.zeros((owners, rp, 128), F32)
        for h in range(part_heads):
            low = lanes >= h * wide
            packed = jnp.where(low & (lanes < 64), top4[:, h], packed)
            packed = jnp.where(lanes >= 64 + h * wide, denom4[:, h], packed)
        side_v[...] = packed
        for ox, oz in itertools.product(range(ngx), range(ngz)):
            if ox or oz:
                px, py, pz = shifted(ox, 0, oz)
                peer = px * ngz + pz
                send(
                    part_v.at[pl.ds(peer * part_heads, part_heads)],
                    prs_v.at[me_owner],
                    p_sem.at[0, peer],
                    p_sem.at[1, me_owner],
                    at(px, py, pz),
                )
                send(
                    side_v.at[peer],
                    srs_v.at[me_owner],
                    s_sem.at[0, peer],
                    s_sem.at[1, me_owner],
                    at(px, py, pz),
                )

    block = (me_owner * part_heads) // heads_dev
    by, bz = block // ngz, lax.rem(block, ngz)
    local = lax.rem(me_owner, heads_dev // part_heads)

    def combine_parts():
        prs_v[me_owner] = part_v[pl.ds(me_owner * part_heads, part_heads)]
        srs_v[me_owner] = side_v[me_owner]
        for ox, oz in itertools.product(range(ngx), range(ngz)):
            if ox or oz:
                px, py, pz = shifted(ox, 0, oz)
                peer = px * ngz + pz
                arrived(prs_v.at[peer], p_sem.at[1, peer])
                arrived(srs_v.at[peer], s_sem.at[1, peer])
        wide = 64 // part_heads

        def column(o, start):
            return jnp.stack(
                [
                    srs_v[o, :, start + h * wide : start + h * wide + 1]
                    for h in range(part_heads)
                ]
            )

        rot = rot_v[pl.ds(me_owner * part_heads, part_heads)]
        newkv = newkv_v[...].astype(BF16).astype(F32)
        own = jnp.sum(rot * newkv[:, :HEAD_DIM], 2, keepdims=True) * scale
        tops = [column(o, 0) for o in range(owners)]
        top = own
        for t in tops:
            top = jnp.maximum(top, t)
        weight = jnp.exp(own - top)
        numer = weight * newkv[:, HEAD_DIM:]
        denom = weight
        for o in range(owners):
            factor = jnp.exp(tops[o] - top)
            numer = numer + factor * prs_v[o].astype(F32)
            denom = denom + factor * column(o, 64)
        rowid = lax.broadcasted_iota(jnp.int32, (part_heads, rp, HEAD_DIM), 1)
        mine = (rowid >= first) & (rowid < first + seq_dev)
        att_v[...] = jnp.where(mine, numer / denom, 0.0).astype(BF16)
        for k in range(ngx):
            px = lax.rem(gx + k, ngx)
            copy = pltpu.make_async_remote_copy(
                src_ref=att_v,
                dst_ref=attall_v.at[gy, local],
                send_sem=a_sem.at[px],
                recv_sem=a_recv.at[gy, local],
                device_id=at(px, by, bz),
                device_id_type=MESH,
            )
            if k:
                copy.start()
                pending.append(copy)
            else:
                same = (by == gy) & (bz == gz)

                @pl.when(same)
                def _():
                    attall_v[gy, local] = att_v[...]

                @pl.when(jnp.logical_not(same))
                def _(copy=copy):
                    copy.start()
                    copy.wait_send()

    def out_product():
        for sy in range(ngy):
            for sl in range(heads_dev // part_heads):
                owner = (gy * ngz + gz) * (heads_dev // part_heads) + sl
                theirs = (sy == gy) & (owner == me_owner)

                @pl.when(jnp.logical_not(theirs))
                def _(sy=sy, sl=sl):
                    arrived(attall_v.at[sy, sl], a_recv.at[sy, sl])

        pieces = []
        for h in range(heads_dev):
            total = attall_v[0, h // part_heads, h % part_heads].astype(F32)
            for sy in range(1, ngy):
                total = total + attall_v[sy, h // part_heads, h % part_heads].astype(F32)
            pieces.append(total.astype(BF16))
        mixed_heads = jnp.concatenate(pieces, 1)
        small[6].wait()
        ct = min(512, dx)
        heads_v[...] = mixed_heads

        @pl.loop(0, dx // ct)
        def _(n):
            columns = pl.ds(pl.multiple_of(n * ct, ct), ct)
            acc_v[:, columns] += jnp.dot(
                heads_v[...], out_v[:, columns], preferred_element_type=F32
            )

    gate_up(0)
    center, inverse = moments()
    gather_query()
    gate_up(1)
    attend()
    gate_up(2)
    combine_parts()
    for step in range(3, ngx):
        gate_up(step)

    g = u = None
    for k in range(ngx):
        peer = lax.rem(gx + k, ngx)
        if k:
            arrived(grs_v.at[peer], g_sem.at[1, peer])
            both = grs_v[peer].astype(F32)
        else:
            both = own_v[...]
        g_part = corrected(both[:rp], both[rows : rows + 1], peer, center)
        u_part = corrected(both[rp:], both[rp + rows : rp + rows + 1], peer, center)
        g = g_part if g is None else g + g_part
        u = u_part if u is None else u + u_part
    g = g * inverse
    u = u * inverse
    hid_v[gx] = (g / (1.0 + jnp.exp(-g)) * u).astype(BF16)
    for k in range(1, ngx):
        peer = lax.rem(gx + k, ngx)
        send(hid_v.at[gx], hid_v.at[gx], h_sem.at[0, peer], h_sem.at[1, gx], at(peer, gy, gz))

    spot = gy * ngz + gz
    ct = min(512, dx // 2)
    half = dx // 2
    peers = [o for o in itertools.product(range(ngy), range(ngz)) if any(o)]

    def down_product(step, low, high):
        source = lax.rem(gx + step, ngx)

        @pl.loop(low // ct, high // ct)
        def _(n):
            columns = pl.ds(pl.multiple_of(n * ct, ct), ct)
            product = jnp.dot(
                hid_v[source], down_v[step, :, columns], preferred_element_type=F32
            )
            if step:
                acc_v[:, columns] += product
            else:
                acc_v[:, columns] = product

    down_copy(0).wait()
    down_product(0, 0, dx)
    out_product()
    for step in range(1, ngx):
        source = lax.rem(gx + step, ngx)
        down_copy(step).wait()
        arrived(hid_v.at[source], h_sem.at[1, source])
        if step < ngx - 1:
            down_product(step, 0, dx)
    for part in range(2):
        down_product(ngx - 1, part * half, (part + 1) * half)
        fin_v[part, spot] = acc_v[:, part * half : (part + 1) * half].astype(BF16)
        for oy, oz in peers:
            px, py, pz = shifted(0, oy, oz)
            peer = py * ngz + pz
            send(
                fin_v.at[part, spot],
                fin_v.at[part, spot],
                f_sem.at[0, part, peer],
                f_sem.at[1, part, spot],
                at(px, py, pz),
            )
    for part in range(2):
        columns = slice(part * half, (part + 1) * half)
        total = x_v[:, columns] + acc_v[:, columns]
        for oy, oz in peers:
            px, py, pz = shifted(0, oy, oz)
            peer = py * ngz + pz
            arrived(fin_v.at[part, peer], f_sem.at[1, part, peer])
            total = total + fin_v[part, peer].astype(F32)
        mixed_ref[:, columns] = total[:rows].astype(BF16)
    for copy in pending:
        copy.wait_send()


def fused(sizes, *args):
    (tokens, gain, qw, kvw, outw, gatew, upw, downw, cache, lengths) = args
    ngx, ngy, ngz = sizes
    rows, dx = tokens.shape
    rp = (rows // 8 + 1) * 8
    qd = qw.shape[1]
    fb = gatew.shape[1] // ngx
    own_heads = qd // HEAD_DIM // ngx
    heads_dev = qd // HEAD_DIM
    owners = ngx * ngz
    part_heads = HEADS // owners
    middle = HEAD_DIM // 2
    spread = (rotary_base ** (-jnp.arange(middle, dtype=F32) / middle)).reshape(1, middle)
    dma = pltpu.SemaphoreType.DMA
    vm = pltpu.VMEM
    scratch = [
        vm(tokens.shape, BF16),
        vm((1, dx), F32),
        vm((1, middle), F32),
        vm(qw.shape, BF16),
        vm(kvw.shape, BF16),
        vm(cache.shape, BF16),
        vm((ngx, dx, fb), BF16),
        vm((ngx, dx, fb), BF16),
        vm(outw.shape, BF16),
        vm((ngx, fb, dx), BF16),
        dma((7,)),
        dma((2, ngx)),
        dma((ngx,)),
        vm((rp, dx), F32),
        vm((rp, dx), BF16),
        vm((ngx, rp, 128), F32),
        vm((ngx, rp, own_heads * HEAD_DIM), F32),
        vm((ngx, rp, own_heads * HEAD_DIM), F32),
        vm((ngx, rp, 2 * HEAD_DIM), F32),
        vm((own_heads, rp, HEAD_DIM), BF16),
        vm((HEADS, rp, HEAD_DIM), BF16),
        vm((HEADS, rp, HEAD_DIM), F32),
        vm((rp, 2 * HEAD_DIM), F32),
        vm((HEADS, rp, HEAD_DIM), BF16),
        vm((owners, part_heads, rp, HEAD_DIM), BF16),
        vm((owners, rp, 128), F32),
        vm((owners, rp, 128), F32),
        vm((part_heads, rp, HEAD_DIM), BF16),
        vm((ngy, heads_dev // part_heads, part_heads, rp, HEAD_DIM), BF16),
        vm((ngx - 1, 2 * rp, fb), BF16),
        vm((ngx, 2 * rp, fb), BF16),
        vm((2 * rp, fb), F32),
        vm((ngx, rp, fb), BF16),
        vm((rp, dx), F32),
        vm((rp, qd), BF16),
        vm((2, ngy * ngz, rp, dx // 2), BF16),
        dma((2, ngx)),
        dma((2, ngx)),
        dma((2, ngx)),
        dma((2, ngx, ngy, ngz)),
        dma((2, owners)),
        dma((2, owners)),
        dma((ngx,)),
        dma((ngy, heads_dev // part_heads)),
        dma((2, ngx)),
        dma((2, ngx)),
        dma((2, 2, ngy * ngz)),
    ]
    anywhere = pl.BlockSpec(memory_space=pl.ANY)
    return pl.pallas_call(
        functools.partial(kernel, (ngx, ngy, ngz, rows, rp)),
        out_shape=(
            pltpu.VMEM(tokens.shape, BF16),
            pltpu.VMEM((cache.shape[0], 2 * HEAD_DIM), BF16),
        ),
        in_specs=[pl.BlockSpec(memory_space=pltpu.SMEM)] + [anywhere] * 10,
        out_specs=(pl.BlockSpec(memory_space=pltpu.VMEM),) * 2,
        scratch_shapes=scratch,
        compiler_params=pltpu.CompilerParams(
            collective_id=0, has_side_effects=True, vmem_limit_bytes=61 * 2**20
        ),
    )(lengths, tokens, gain.reshape(1, dx), spread, qw, kvw, cache, gatew, upw, outw, downw)


def fits(sizes, d_dev, q_dev, ff_dev, weight_bytes):
    ngx, ngy, ngz = sizes
    heads_dev = q_dev // HEAD_DIM
    return (
        ngx >= 3
        and HEADS // (ngx * ngz) in (1, 2, 4)
        and d_dev % 1024 == 0
        and heads_dev % ngx == 0
        and HEADS % (ngx * ngz) == 0
        and heads_dev % (HEADS // (ngx * ngz)) == 0
        and ff_dev % (ngx * 128) == 0
        and weight_bytes <= 60 * 2**20
    )


def choose(sizes, *args):
    held = sum(a.size * a.dtype.itemsize for a in args[2:9])
    if fits(sizes, args[0].shape[1], args[2].shape[1], args[5].shape[1], held):
        return fused(sizes, *args)
    return body(*args)


def solution(mesh):
    sizes = tuple(mesh.shape[a] for a in ("gx", "gy", "gz"))
    chosen = functools.partial(choose, sizes)
    in_specs = (
        P("group", "gx"),
        P("gx"),
        P("gx", ("gy", "gz")),
        P("gx", None),
        P(("gy", "gz"), "gx"),
        P("gx", ("gy", "gz")),
        P("gx", ("gy", "gz")),
        P(("gy", "gz"), "gx"),
        P(("group", "gy"), ("gx", "gz"), None),
        P(("group", "gy")),
    )
    out_specs = (P("group", "gx"), P(("group", "gy"), None))
    return jax.shard_map(chosen, mesh=mesh, in_specs=in_specs, out_specs=out_specs, check_vma=False)
```

```python
import functools
import itertools

import jax
import jax.numpy as jnp
import numpy as np
from jax import lax
from jax.experimental import pallas as pl
from jax.experimental.pallas import tpu as pltpu
from jax.sharding import PartitionSpec as P

D = 8192
HEADS = 16
HEAD_DIM = 256


epsilon = 1e-05
masked_fill = -1e30
rotary_base = 10000.0


def joined(part, axis, combine):
    gathered = jax.tree.map(lambda a: lax.all_gather(a, axis), part)

    def take(source):
        return jax.tree.map(lambda a: lax.dynamic_index_in_dim(a, source, 0, False), gathered)

    return lax.fori_loop(
        1, lax.axis_size(axis), lambda source, state: combine(state, take(source)), take(0)
    )


def rotate(values, angle):
    middle = values.shape[-1] // 2
    first = values[..., :middle]
    second = values[..., middle:]
    cosine = jnp.cos(angle)
    sine_part = jnp.sin(angle)
    return jnp.concatenate(
        [first * cosine - second * sine_part, first * sine_part + second * cosine], -1
    )


def angles(lengths, head_dim):
    middle = head_dim // 2
    spread = rotary_base ** (-jnp.arange(middle, dtype=jnp.float32) / middle)
    return lengths.astype(jnp.float32)[:, None] * spread[None, :]


def combine(earlier, later):
    top = jnp.maximum(earlier[0], later[0])
    first_scale = jnp.exp(earlier[0] - top)
    second_scale = jnp.exp(later[0] - top)
    numer = earlier[1] * first_scale[..., None] + later[1] * second_scale[..., None]
    denom = earlier[2] * first_scale + later[2] * second_scale
    return (top, numer, denom)


def body(
    tokens,
    norm_gain,
    q_weight,
    kv_weight,
    out_weight,
    gate_weight,
    up_weight,
    down_weight,
    kv_cache,
    lengths,
):
    inputs = tokens.astype(jnp.float32)
    totals = lax.psum((jnp.sum(inputs, 1), jnp.sum(inputs * inputs, 1)), "gx")
    center = totals[0] / D
    spread_sq = totals[1] / D - center * center
    normed = (
        (inputs - center[:, None]) * lax.rsqrt(spread_sq + epsilon)[:, None] * norm_gain[None, :]
    ).astype(jnp.bfloat16)
    query_part = jnp.dot(normed, q_weight, preferred_element_type=jnp.float32)
    keyval_part = jnp.dot(normed, kv_weight, preferred_element_type=jnp.float32)
    gate_part = jnp.dot(normed, gate_weight, preferred_element_type=jnp.float32)
    up_part = jnp.dot(normed, up_weight, preferred_element_type=jnp.float32)
    query, keyval, gate, upward = lax.psum((query_part, keyval_part, gate_part, up_part), "gx")
    hidden = (jax.nn.silu(gate) * upward).astype(jnp.bfloat16)
    seq_dev = lengths.shape[0]
    row_groups = lax.axis_size("gy")
    block = q_weight.shape[1]
    first_row = lax.axis_index("gy") * seq_dev
    angle = angles(lengths, HEAD_DIM)
    own_keyval = lax.dynamic_slice_in_dim(keyval, first_row, seq_dev, 0)
    new_kv = jnp.concatenate(
        [rotate(own_keyval[:, :HEAD_DIM], angle), own_keyval[:, HEAD_DIM:]], 1
    ).astype(jnp.bfloat16)
    query_bf = query.astype(jnp.bfloat16)
    every_head = lax.all_gather(query_bf, ("gy", "gz"), axis=1, tiled=True)
    own_query = lax.dynamic_slice_in_dim(every_head, first_row, seq_dev, 0)
    rotated = rotate(
        own_query.astype(jnp.float32).reshape(seq_dev, HEADS, HEAD_DIM), angle[:, None, :]
    ).astype(jnp.bfloat16)
    ctx_dev = kv_cache.shape[1]
    offset = lax.axis_index(("gx", "gz")) * ctx_dev
    positions = offset + jnp.arange(ctx_dev, dtype=jnp.int32)
    live = positions[None, :] < lengths[:, None]
    scale = HEAD_DIM ** (-0.5)
    scores = (
        jnp.einsum(
            "shd,scd->shc", rotated, kv_cache[:, :, :HEAD_DIM], preferred_element_type=jnp.float32
        )
        * scale
    )
    key_new = new_kv[:, :HEAD_DIM]
    value_new = new_kv[:, HEAD_DIM:]
    own_score = (
        jnp.einsum("shd,sd->sh", rotated, key_new, preferred_element_type=jnp.float32) * scale
    )
    hidden_scores = jnp.where(live[:, None, :], scores, masked_fill)
    local_top = jnp.maximum(jnp.max(hidden_scores, 2), own_score)
    weights = jnp.where(live[:, None, :], jnp.exp(hidden_scores - local_top[..., None]), 0.0)
    numer = jnp.einsum(
        "shc,scd->shd",
        weights.astype(jnp.bfloat16),
        kv_cache[:, :, HEAD_DIM:],
        preferred_element_type=jnp.float32,
    )
    denom = jnp.sum(weights, 2)
    top, numer, denom = joined((local_top, numer, denom), ("gx", "gz"), combine)
    own_weight = jnp.exp(own_score - top)
    numer = numer + own_weight[..., None] * value_new.astype(jnp.float32)[:, None, :]
    denom = denom + own_weight
    attended = (numer / denom[..., None]).astype(jnp.bfloat16)
    grouped = attended.reshape(seq_dev, row_groups, HEADS * HEAD_DIM // row_groups)
    picked = lax.dynamic_slice_in_dim(grouped, lax.axis_index("gz") * block, block, 2)
    head_block = lax.all_to_all(picked, "gy", split_axis=1, concat_axis=0, tiled=True).reshape(
        seq_dev * row_groups, block
    )
    partial_value = jnp.dot(head_block, out_weight, preferred_element_type=jnp.float32) + jnp.dot(
        hidden, down_weight, preferred_element_type=jnp.float32
    )
    total = lax.psum(partial_value, ("gy", "gz"))
    mixed = (inputs + total).astype(jnp.bfloat16)
    return (mixed, new_kv)


MESH = pl.DeviceIdType.MESH
F32 = jnp.float32
BF16 = jnp.bfloat16


def kernel(
    dims,
    lengths_ref,
    tokens_h,
    gain_h,
    spread_h,
    q_h,
    kv_h,
    cache_h,
    gate_h,
    up_h,
    out_h,
    down_h,
    mixed_ref,
    newkv_ref,
    tokens_v,
    gain_v,
    spread_v,
    q_v,
    kv_v,
    cache_v,
    gate_v,
    up_v,
    out_v,
    down_v,
    load_sem,
    gu_sem,
    down_sem,
    x_v,
    normed_v,
    stat_v,
    qp_v,
    qrs_v,
    kvs_v,
    qsend_v,
    qall_v,
    rot_v,
    newkv_v,
    part_v,
    prs_v,
    side_v,
    srs_v,
    att_v,
    attall_v,
    gsend_v,
    grs_v,
    own_v,
    hid_v,
    acc_v,
    heads_v,
    fin_v,
    stat_sem,
    q_sem,
    kvx_sem,
    qa_sem,
    p_sem,
    s_sem,
    a_sem,
    a_recv,
    g_sem,
    h_sem,
    f_sem,
):
    ngx, ngy, ngz, rows, rp = dims
    gx, gy, gz = lax.axis_index("gx"), lax.axis_index("gy"), lax.axis_index("gz")
    dx = x_v.shape[1]
    qd = q_v.shape[1]
    heads_dev = qd // HEAD_DIM
    own_heads = heads_dev // ngx
    seq_dev = cache_v.shape[0]
    ctx_dev = cache_v.shape[1]
    fb = gate_v.shape[2]
    owners = ngx * ngz
    part_heads = HEADS // owners
    first = gy * seq_dev
    scale = HEAD_DIM ** (-0.5)
    middle = HEAD_DIM // 2

    small = [
        pltpu.make_async_copy(a, b, load_sem.at[i])
        for i, (a, b) in enumerate(
            (
                (tokens_h, tokens_v),
                (gain_h, gain_v),
                (spread_h, spread_v),
                (q_h, q_v),
                (kv_h, kv_v),
                (cache_h, cache_v),
                (out_h, out_v),
            )
        )
    ]

    def gu_copies(step):
        block = lax.rem(gx + 1 + step, ngx)
        columns = pl.ds(pl.multiple_of(block * fb, fb), fb)
        return (
            pltpu.make_async_copy(gate_h.at[:, columns], gate_v.at[step], gu_sem.at[0, step]),
            pltpu.make_async_copy(up_h.at[:, columns], up_v.at[step], gu_sem.at[1, step]),
        )

    def down_copy(step):
        block = lax.rem(gx + step, ngx)
        picked = pl.ds(pl.multiple_of(block * fb, fb), fb)
        return pltpu.make_async_copy(down_h.at[picked], down_v.at[step], down_sem.at[step])

    offsets = [o for o in itertools.product(range(ngx), range(ngy), range(ngz)) if any(o)]

    def shifted(ox, oy, oz):
        return lax.rem(gx + ox, ngx), lax.rem(gy + oy, ngy), lax.rem(gz + oz, ngz)

    def at(px, py, pz):
        return {"gx": px, "gy": py, "gz": pz}

    barrier = pltpu.get_barrier_semaphore()
    for offset in offsets:
        pl.semaphore_signal(barrier, inc=1, device_id=at(*shifted(*offset)), device_id_type=MESH)

    for copy in small[:6]:
        copy.start()
    for step in range(ngx):
        for copy in gu_copies(step):
            copy.start()
    small[6].start()
    for step in range(ngx):
        down_copy(step).start()

    small[0].wait()
    x_v[...] = jnp.zeros_like(x_v)
    x_v[0:rows, :] = tokens_v[...].astype(F32)
    x = x_v[...]
    lane = lax.broadcasted_iota(jnp.int32, (rp, 128), 1)
    stat_v[gx] = jnp.where(
        lane < 64, jnp.sum(x, 1, keepdims=True), jnp.sum(x * x, 1, keepdims=True)
    )
    small[1].wait()
    spare = lax.broadcasted_iota(jnp.int32, (rp, dx), 0) == rows
    local_mean = stat_v[gx][:, 0:1] / dx
    centred = jnp.where(spare, 1.0, x - local_mean)
    normed_v[...] = (centred * gain_v[...]).astype(BF16)

    qo = own_heads * HEAD_DIM
    small[3].wait()

    @pl.loop(0, ngx)
    def _(j):
        columns = pl.ds(pl.multiple_of(j * qo, qo), qo)
        qp_v[j] = jnp.dot(normed_v[...], q_v[:, columns], preferred_element_type=F32)

    pl.semaphore_wait(barrier, len(offsets))

    pending = []

    def send(source, target, sends, receives, device):
        copy = pltpu.make_async_remote_copy(
            src_ref=source,
            dst_ref=target,
            send_sem=sends,
            recv_sem=receives,
            device_id=device,
            device_id_type=MESH,
        )
        copy.start()
        pending.append(copy)

    def arrived(slot, receives):
        pltpu.make_async_remote_copy(
            src_ref=slot,
            dst_ref=slot,
            send_sem=receives,
            recv_sem=receives,
            device_id=at(gx, gy, gz),
            device_id_type=MESH,
        ).wait_recv()

    for k in range(1, ngx):
        peer = lax.rem(gx + k, ngx)
        send(stat_v.at[gx], stat_v.at[gx], stat_sem.at[0, peer], stat_sem.at[1, gx], at(peer, gy, gz))
        send(qp_v.at[peer], qrs_v.at[gx], q_sem.at[0, peer], q_sem.at[1, gx], at(peer, gy, gz))
    small[4].wait()
    kvs_v[gx] = jnp.dot(normed_v[...], kv_v[...], preferred_element_type=F32)
    for k in range(1, ngx):
        peer = lax.rem(gx + k, ngx)
        send(kvs_v.at[gx], kvs_v.at[gx], kvx_sem.at[0, peer], kvx_sem.at[1, gx], at(peer, gy, gz))
    small[2].wait()

    row = lax.broadcasted_iota(jnp.int32, (rp, middle), 0)
    length = jnp.zeros((rp, middle), jnp.int32)
    for s in range(seq_dev):
        length = jnp.where(row == first + s, lengths_ref[s], length)
    angle = length.astype(F32) * spread_v[...]
    cosine = jnp.cos(angle)
    sine = jnp.sin(angle)

    def moments():
        for k in range(1, ngx):
            peer = lax.rem(gx + k, ngx)
            arrived(stat_v.at[peer], stat_sem.at[1, peer])
        totals = stat_v[0]
        for k in range(1, ngx):
            totals = totals + stat_v[k]
        center = totals[:, 0:1] / D
        spread_sq = totals[:, 64:65] / D - center * center
        return center, lax.rsqrt(spread_sq + epsilon)

    def corrected(part, gain_row, source, center):
        return part + (stat_v[source][:, 0:1] / dx - center) * gain_row

    tile = min(512, fb)

    def gate_up(step):
        for copy in gu_copies(step):
            copy.wait()

        @pl.loop(0, fb // tile)
        def _(n):
            columns = pl.ds(pl.multiple_of(n * tile, tile), tile)
            g = jnp.dot(normed_v[...], gate_v[step, :, columns], preferred_element_type=F32)
            u = jnp.dot(normed_v[...], up_v[step, :, columns], preferred_element_type=F32)
            both = jnp.concatenate([g, u], 0)
            if step < ngx - 1:
                gsend_v[step, :, columns] = both.astype(BF16)
            else:
                own_v[:, columns] = both

        if step < ngx - 1:
            peer = lax.rem(gx + 1 + step, ngx)
            send(gsend_v.at[step], grs_v.at[gx], g_sem.at[0, peer], g_sem.at[1, gx], at(peer, gy, gz))

    def gather_query():
        qrs_v[gx] = qp_v[gx]
        total = None
        for k in range(ngx):
            peer = lax.rem(gx + k, ngx)
            if k:
                arrived(qrs_v.at[peer], q_sem.at[1, peer])
            part = corrected(qrs_v[peer], qrs_v[peer, rows : rows + 1, :], peer, center)
            total = part if total is None else total + part
        total = total * inverse
        mine = (gy * ngz + gz) * heads_dev + gx * own_heads
        for h in range(own_heads):
            piece = total[:, h * HEAD_DIM : (h + 1) * HEAD_DIM].astype(BF16)
            qsend_v[h] = piece
            qall_v[mine + h] = piece
        for offset in offsets:
            px, py, pz = shifted(*offset)
            send(
                qsend_v,
                qall_v.at[pl.ds(mine, own_heads)],
                qa_sem.at[0, px, py, pz],
                qa_sem.at[1, gx, gy, gz],
                at(px, py, pz),
            )

    me_owner = gx * ngz + gz

    def attend():
        keyval = None
        for k in range(ngx):
            peer = lax.rem(gx + k, ngx)
            if k:
                arrived(kvs_v.at[peer], kvx_sem.at[1, peer])
            part = corrected(kvs_v[peer], kvs_v[peer, rows : rows + 1, :], peer, center)
            keyval = part if keyval is None else keyval + part
        keyval = keyval * inverse
        a = keyval[:, :middle]
        b = keyval[:, middle:HEAD_DIM]
        newkv_v[:, :middle] = a * cosine - b * sine
        newkv_v[:, middle:HEAD_DIM] = a * sine + b * cosine
        newkv_v[:, HEAD_DIM:] = keyval[:, HEAD_DIM:]
        picked = newkv_v[0:seq_dev, :]
        for y in range(1, ngy):
            picked = jnp.where(gy == y, newkv_v[y * seq_dev : (y + 1) * seq_dev, :], picked)
        newkv_ref[...] = picked.astype(BF16)
        for offset in offsets:
            px, py, pz = shifted(*offset)
            slot = (py * ngz + pz) * heads_dev + px * own_heads
            arrived(qall_v.at[pl.ds(slot, own_heads)], qa_sem.at[1, px, py, pz])
        q3 = qall_v[...].astype(F32)
        a = q3[:, :, :middle]
        b = q3[:, :, middle:]
        rot_v[:, :, :middle] = (a * cosine - b * sine).astype(BF16).astype(F32)
        rot_v[:, :, middle:] = (a * sine + b * cosine).astype(BF16).astype(F32)
        small[5].wait()
        rotated = rot_v[...].reshape(HEADS * rp, HEAD_DIM).astype(BF16)
        rowid = lax.rem(lax.broadcasted_iota(jnp.int32, (HEADS * rp, ctx_dev), 0), rp)
        position = (gx * ngz + gz) * ctx_dev + lax.broadcasted_iota(
            jnp.int32, (HEADS * rp, ctx_dev), 1
        )
        scores = jnp.full((HEADS * rp, ctx_dev), masked_fill, F32)
        limit = jnp.zeros((HEADS * rp, ctx_dev), jnp.int32)
        for s in range(seq_dev):
            raw = lax.dot_general(
                rotated,
                cache_v[s, :, :HEAD_DIM],
                (((1,), (1,)), ((), ())),
                preferred_element_type=F32,
            )
            limit = jnp.where(rowid == first + s, lengths_ref[s], limit)
            scores = jnp.where(rowid == first + s, raw * scale, scores)
        live = position < limit
        scores = jnp.where(live, scores, masked_fill)
        top = jnp.max(scores, 1, keepdims=True)
        weights = jnp.where(live, jnp.exp(scores - top), 0.0)
        denom = jnp.sum(weights, 1, keepdims=True)
        numer = jnp.zeros((HEADS * rp, HEAD_DIM), F32)
        for s in range(seq_dev):
            numer = numer + jnp.dot(
                jnp.where(rowid == first + s, weights, 0.0).astype(BF16),
                cache_v[s, :, HEAD_DIM:],
                preferred_element_type=F32,
            )
        part_v[...] = numer.reshape(HEADS, rp, HEAD_DIM).astype(BF16)
        wide = 64 // part_heads
        lanes = lax.broadcasted_iota(jnp.int32, (owners, rp, 128), 2)
        top4 = jnp.broadcast_to(top, (HEADS * rp, 128)).reshape(owners, part_heads, rp, 128)
        denom4 = jnp.broadcast_to(denom, (HEADS * rp, 128)).reshape(owners, part_heads, rp, 128)
        packed = jnp.zeros((owners, rp, 128), F32)
        for h in range(part_heads):
            low = lanes >= h * wide
            packed = jnp.where(low & (lanes < 64), top4[:, h], packed)
            packed = jnp.where(lanes >= 64 + h * wide, denom4[:, h], packed)
        side_v[...] = packed
        for ox, oz in itertools.product(range(ngx), range(ngz)):
            if ox or oz:
                px, py, pz = shifted(ox, 0, oz)
                peer = px * ngz + pz
                send(
                    part_v.at[pl.ds(peer * part_heads, part_heads)],
                    prs_v.at[me_owner],
                    p_sem.at[0, peer],
                    p_sem.at[1, me_owner],
                    at(px, py, pz),
                )
                send(
                    side_v.at[peer],
                    srs_v.at[me_owner],
                    s_sem.at[0, peer],
                    s_sem.at[1, me_owner],
                    at(px, py, pz),
                )

    block = (me_owner * part_heads) // heads_dev
    by, bz = block // ngz, lax.rem(block, ngz)
    local = lax.rem(me_owner, heads_dev // part_heads)

    def combine_parts():
        prs_v[me_owner] = part_v[pl.ds(me_owner * part_heads, part_heads)]
        srs_v[me_owner] = side_v[me_owner]
        for ox, oz in itertools.product(range(ngx), range(ngz)):
            if ox or oz:
                px, py, pz = shifted(ox, 0, oz)
                peer = px * ngz + pz
                arrived(prs_v.at[peer], p_sem.at[1, peer])
                arrived(srs_v.at[peer], s_sem.at[1, peer])
        wide = 64 // part_heads

        def column(o, start):
            return jnp.stack(
                [
                    srs_v[o, :, start + h * wide : start + h * wide + 1]
                    for h in range(part_heads)
                ]
            )

        rot = rot_v[pl.ds(me_owner * part_heads, part_heads)]
        newkv = newkv_v[...].astype(BF16).astype(F32)
        own = jnp.sum(rot * newkv[:, :HEAD_DIM], 2, keepdims=True) * scale
        tops = [column(o, 0) for o in range(owners)]
        top = own
        for t in tops:
            top = jnp.maximum(top, t)
        weight = jnp.exp(own - top)
        numer = weight * newkv[:, HEAD_DIM:]
        denom = weight
        for o in range(owners):
            factor = jnp.exp(tops[o] - top)
            numer = numer + factor * prs_v[o].astype(F32)
            denom = denom + factor * column(o, 64)
        rowid = lax.broadcasted_iota(jnp.int32, (part_heads, rp, HEAD_DIM), 1)
        mine = (rowid >= first) & (rowid < first + seq_dev)
        att_v[...] = jnp.where(mine, numer / denom, 0.0).astype(BF16)
        for k in range(ngx):
            px = lax.rem(gx + k, ngx)
            copy = pltpu.make_async_remote_copy(
                src_ref=att_v,
                dst_ref=attall_v.at[gy, local],
                send_sem=a_sem.at[px],
                recv_sem=a_recv.at[gy, local],
                device_id=at(px, by, bz),
                device_id_type=MESH,
            )
            if k:
                copy.start()
                pending.append(copy)
            else:
                same = (by == gy) & (bz == gz)

                @pl.when(same)
                def _():
                    attall_v[gy, local] = att_v[...]

                @pl.when(jnp.logical_not(same))
                def _(copy=copy):
                    copy.start()
                    copy.wait_send()

    def gather_heads():
        for sy in range(ngy):
            for sl in range(heads_dev // part_heads):
                owner = (gy * ngz + gz) * (heads_dev // part_heads) + sl
                theirs = (sy == gy) & (owner == me_owner)

                @pl.when(jnp.logical_not(theirs))
                def _(sy=sy, sl=sl):
                    arrived(attall_v.at[sy, sl], a_recv.at[sy, sl])

        pieces = []
        for h in range(heads_dev):
            total = attall_v[0, h // part_heads, h % part_heads].astype(F32)
            for sy in range(1, ngy):
                total = total + attall_v[sy, h // part_heads, h % part_heads].astype(F32)
            pieces.append(total.astype(BF16))
        mixed_heads = jnp.concatenate(pieces, 1)
        small[6].wait()
        heads_v[...] = mixed_heads

    def out_product(low, high):
        @pl.loop(low // ct, high // ct)
        def _(n):
            columns = pl.ds(pl.multiple_of(n * ct, ct), ct)
            acc_v[:, columns] += jnp.dot(
                heads_v[...], out_v[:, columns], preferred_element_type=F32
            )

    gate_up(0)
    center, inverse = moments()
    gather_query()
    for step in range(1, ngx - 1):
        gate_up(step)
    attend()
    gate_up(ngx - 1)

    g = u = None
    for k in range(ngx):
        peer = lax.rem(gx + k, ngx)
        if k:
            arrived(grs_v.at[peer], g_sem.at[1, peer])
            both = grs_v[peer].astype(F32)
        else:
            both = own_v[...]
        g_part = corrected(both[:rp], both[rows : rows + 1], peer, center)
        u_part = corrected(both[rp:], both[rp + rows : rp + rows + 1], peer, center)
        g = g_part if g is None else g + g_part
        u = u_part if u is None else u + u_part
    g = g * inverse
    u = u * inverse
    hid_v[gx] = (g / (1.0 + jnp.exp(-g)) * u).astype(BF16)
    for k in range(1, ngx):
        peer = lax.rem(gx + k, ngx)
        send(hid_v.at[gx], hid_v.at[gx], h_sem.at[0, peer], h_sem.at[1, gx], at(peer, gy, gz))

    combine_parts()
    spot = gy * ngz + gz
    ct = min(512, dx // 2)
    half = dx // 2
    peers = [o for o in itertools.product(range(ngy), range(ngz)) if any(o)]

    def down_product(step, low, high):
        source = lax.rem(gx + step, ngx)

        @pl.loop(low // ct, high // ct)
        def _(n):
            columns = pl.ds(pl.multiple_of(n * ct, ct), ct)
            product = jnp.dot(
                hid_v[source], down_v[step, :, columns], preferred_element_type=F32
            )
            if step:
                acc_v[:, columns] += product
            else:
                acc_v[:, columns] = product

    for step in range(ngx):
        source = lax.rem(gx + step, ngx)
        down_copy(step).wait()
        if step:
            arrived(hid_v.at[source], h_sem.at[1, source])
        down_product(step, 0, dx)
    gather_heads()
    for part in range(2):
        out_product(part * half, (part + 1) * half)
        fin_v[part, spot] = acc_v[:, part * half : (part + 1) * half].astype(BF16)
        for oy, oz in peers:
            px, py, pz = shifted(0, oy, oz)
            peer = py * ngz + pz
            send(
                fin_v.at[part, spot],
                fin_v.at[part, spot],
                f_sem.at[0, part, peer],
                f_sem.at[1, part, spot],
                at(px, py, pz),
            )
    for part in range(2):
        columns = slice(part * half, (part + 1) * half)
        total = x_v[:, columns] + acc_v[:, columns]
        for oy, oz in peers:
            px, py, pz = shifted(0, oy, oz)
            peer = py * ngz + pz
            arrived(fin_v.at[part, peer], f_sem.at[1, part, peer])
            total = total + fin_v[part, peer].astype(F32)
        mixed_ref[:, columns] = total[:rows].astype(BF16)
    for copy in pending:
        copy.wait_send()


def fused(sizes, *args):
    (tokens, gain, qw, kvw, outw, gatew, upw, downw, cache, lengths) = args
    ngx, ngy, ngz = sizes
    rows, dx = tokens.shape
    rp = (rows // 8 + 1) * 8
    qd = qw.shape[1]
    fb = gatew.shape[1] // ngx
    own_heads = qd // HEAD_DIM // ngx
    heads_dev = qd // HEAD_DIM
    owners = ngx * ngz
    part_heads = HEADS // owners
    middle = HEAD_DIM // 2
    spread = np.power(
        np.float32(rotary_base), -np.arange(middle, dtype=np.float32) / np.float32(middle)
    ).reshape(1, middle)
    dma = pltpu.SemaphoreType.DMA
    vm = pltpu.VMEM
    scratch = [
        vm(tokens.shape, BF16),
        vm((1, dx), F32),
        vm((1, middle), F32),
        vm(qw.shape, BF16),
        vm(kvw.shape, BF16),
        vm(cache.shape, BF16),
        vm((ngx, dx, fb), BF16),
        vm((ngx, dx, fb), BF16),
        vm(outw.shape, BF16),
        vm((ngx, fb, dx), BF16),
        dma((7,)),
        dma((2, ngx)),
        dma((ngx,)),
        vm((rp, dx), F32),
        vm((rp, dx), BF16),
        vm((ngx, rp, 128), F32),
        vm((ngx, rp, own_heads * HEAD_DIM), F32),
        vm((ngx, rp, own_heads * HEAD_DIM), F32),
        vm((ngx, rp, 2 * HEAD_DIM), F32),
        vm((own_heads, rp, HEAD_DIM), BF16),
        vm((HEADS, rp, HEAD_DIM), BF16),
        vm((HEADS, rp, HEAD_DIM), F32),
        vm((rp, 2 * HEAD_DIM), F32),
        vm((HEADS, rp, HEAD_DIM), BF16),
        vm((owners, part_heads, rp, HEAD_DIM), BF16),
        vm((owners, rp, 128), F32),
        vm((owners, rp, 128), F32),
        vm((part_heads, rp, HEAD_DIM), BF16),
        vm((ngy, heads_dev // part_heads, part_heads, rp, HEAD_DIM), BF16),
        vm((ngx - 1, 2 * rp, fb), BF16),
        vm((ngx, 2 * rp, fb), BF16),
        vm((2 * rp, fb), F32),
        vm((ngx, rp, fb), BF16),
        vm((rp, dx), F32),
        vm((rp, qd), BF16),
        vm((2, ngy * ngz, rp, dx // 2), BF16),
        dma((2, ngx)),
        dma((2, ngx)),
        dma((2, ngx)),
        dma((2, ngx, ngy, ngz)),
        dma((2, owners)),
        dma((2, owners)),
        dma((ngx,)),
        dma((ngy, heads_dev // part_heads)),
        dma((2, ngx)),
        dma((2, ngx)),
        dma((2, 2, ngy * ngz)),
    ]
    anywhere = pl.BlockSpec(memory_space=pl.ANY)
    return pl.pallas_call(
        functools.partial(kernel, (ngx, ngy, ngz, rows, rp)),
        out_shape=(
            pltpu.VMEM(tokens.shape, BF16),
            pltpu.VMEM((cache.shape[0], 2 * HEAD_DIM), BF16),
        ),
        in_specs=[pl.BlockSpec(memory_space=pltpu.SMEM)] + [anywhere] * 10,
        out_specs=(pl.BlockSpec(memory_space=pltpu.VMEM),) * 2,
        scratch_shapes=scratch,
        compiler_params=pltpu.CompilerParams(
            collective_id=0, has_side_effects=True, vmem_limit_bytes=61 * 2**20
        ),
    )(lengths, tokens, gain.reshape(1, dx), spread, qw, kvw, cache, gatew, upw, outw, downw)


def fits(sizes, d_dev, q_dev, ff_dev, weight_bytes):
    ngx, ngy, ngz = sizes
    heads_dev = q_dev // HEAD_DIM
    return (
        ngx >= 3
        and HEADS // (ngx * ngz) in (1, 2, 4)
        and d_dev % 1024 == 0
        and heads_dev % ngx == 0
        and HEADS % (ngx * ngz) == 0
        and heads_dev % (HEADS // (ngx * ngz)) == 0
        and ff_dev % (ngx * 128) == 0
        and weight_bytes <= 60 * 2**20
    )


def choose(sizes, *args):
    held = sum(a.size * a.dtype.itemsize for a in args[2:9])
    if fits(sizes, args[0].shape[1], args[2].shape[1], args[5].shape[1], held):
        return fused(sizes, *args)
    return body(*args)


def solution(mesh):
    sizes = tuple(mesh.shape[a] for a in ("gx", "gy", "gz"))
    chosen = functools.partial(choose, sizes)
    in_specs = (
        P("group", "gx"),
        P("gx"),
        P("gx", ("gy", "gz")),
        P("gx", None),
        P(("gy", "gz"), "gx"),
        P("gx", ("gy", "gz")),
        P("gx", ("gy", "gz")),
        P(("gy", "gz"), "gx"),
        P(("group", "gy"), ("gx", "gz"), None),
        P(("group", "gy")),
    )
    out_specs = (P("group", "gx"), P(("group", "gy"), None))
    return jax.shard_map(chosen, mesh=mesh, in_specs=in_specs, out_specs=out_specs, check_vma=False)
```

```python
import functools
import itertools

import jax
import jax.numpy as jnp
import numpy as np
from jax import lax
from jax.experimental import pallas as pl
from jax.experimental.pallas import tpu as pltpu
from jax.sharding import PartitionSpec as P

D = 8192
HEADS = 16
HEAD_DIM = 256


epsilon = 1e-05
masked_fill = -1e30
rotary_base = 10000.0


def joined(part, axis, combine):
    gathered = jax.tree.map(lambda a: lax.all_gather(a, axis), part)

    def take(source):
        return jax.tree.map(lambda a: lax.dynamic_index_in_dim(a, source, 0, False), gathered)

    return lax.fori_loop(
        1, lax.axis_size(axis), lambda source, state: combine(state, take(source)), take(0)
    )


def rotate(values, angle):
    middle = values.shape[-1] // 2
    first = values[..., :middle]
    second = values[..., middle:]
    cosine = jnp.cos(angle)
    sine_part = jnp.sin(angle)
    return jnp.concatenate(
        [first * cosine - second * sine_part, first * sine_part + second * cosine], -1
    )


def angles(lengths, head_dim):
    middle = head_dim // 2
    spread = rotary_base ** (-jnp.arange(middle, dtype=jnp.float32) / middle)
    return lengths.astype(jnp.float32)[:, None] * spread[None, :]


def combine(earlier, later):
    top = jnp.maximum(earlier[0], later[0])
    first_scale = jnp.exp(earlier[0] - top)
    second_scale = jnp.exp(later[0] - top)
    numer = earlier[1] * first_scale[..., None] + later[1] * second_scale[..., None]
    denom = earlier[2] * first_scale + later[2] * second_scale
    return (top, numer, denom)


def body(
    tokens,
    norm_gain,
    q_weight,
    kv_weight,
    out_weight,
    gate_weight,
    up_weight,
    down_weight,
    kv_cache,
    lengths,
):
    inputs = tokens.astype(jnp.float32)
    totals = lax.psum((jnp.sum(inputs, 1), jnp.sum(inputs * inputs, 1)), "gx")
    center = totals[0] / D
    spread_sq = totals[1] / D - center * center
    normed = (
        (inputs - center[:, None]) * lax.rsqrt(spread_sq + epsilon)[:, None] * norm_gain[None, :]
    ).astype(jnp.bfloat16)
    query_part = jnp.dot(normed, q_weight, preferred_element_type=jnp.float32)
    keyval_part = jnp.dot(normed, kv_weight, preferred_element_type=jnp.float32)
    gate_part = jnp.dot(normed, gate_weight, preferred_element_type=jnp.float32)
    up_part = jnp.dot(normed, up_weight, preferred_element_type=jnp.float32)
    query, keyval, gate, upward = lax.psum((query_part, keyval_part, gate_part, up_part), "gx")
    hidden = (jax.nn.silu(gate) * upward).astype(jnp.bfloat16)
    seq_dev = lengths.shape[0]
    row_groups = lax.axis_size("gy")
    block = q_weight.shape[1]
    first_row = lax.axis_index("gy") * seq_dev
    angle = angles(lengths, HEAD_DIM)
    own_keyval = lax.dynamic_slice_in_dim(keyval, first_row, seq_dev, 0)
    new_kv = jnp.concatenate(
        [rotate(own_keyval[:, :HEAD_DIM], angle), own_keyval[:, HEAD_DIM:]], 1
    ).astype(jnp.bfloat16)
    query_bf = query.astype(jnp.bfloat16)
    every_head = lax.all_gather(query_bf, ("gy", "gz"), axis=1, tiled=True)
    own_query = lax.dynamic_slice_in_dim(every_head, first_row, seq_dev, 0)
    rotated = rotate(
        own_query.astype(jnp.float32).reshape(seq_dev, HEADS, HEAD_DIM), angle[:, None, :]
    ).astype(jnp.bfloat16)
    ctx_dev = kv_cache.shape[1]
    offset = lax.axis_index(("gx", "gz")) * ctx_dev
    positions = offset + jnp.arange(ctx_dev, dtype=jnp.int32)
    live = positions[None, :] < lengths[:, None]
    scale = HEAD_DIM ** (-0.5)
    scores = (
        jnp.einsum(
            "shd,scd->shc", rotated, kv_cache[:, :, :HEAD_DIM], preferred_element_type=jnp.float32
        )
        * scale
    )
    key_new = new_kv[:, :HEAD_DIM]
    value_new = new_kv[:, HEAD_DIM:]
    own_score = (
        jnp.einsum("shd,sd->sh", rotated, key_new, preferred_element_type=jnp.float32) * scale
    )
    hidden_scores = jnp.where(live[:, None, :], scores, masked_fill)
    local_top = jnp.maximum(jnp.max(hidden_scores, 2), own_score)
    weights = jnp.where(live[:, None, :], jnp.exp(hidden_scores - local_top[..., None]), 0.0)
    numer = jnp.einsum(
        "shc,scd->shd",
        weights.astype(jnp.bfloat16),
        kv_cache[:, :, HEAD_DIM:],
        preferred_element_type=jnp.float32,
    )
    denom = jnp.sum(weights, 2)
    top, numer, denom = joined((local_top, numer, denom), ("gx", "gz"), combine)
    own_weight = jnp.exp(own_score - top)
    numer = numer + own_weight[..., None] * value_new.astype(jnp.float32)[:, None, :]
    denom = denom + own_weight
    attended = (numer / denom[..., None]).astype(jnp.bfloat16)
    grouped = attended.reshape(seq_dev, row_groups, HEADS * HEAD_DIM // row_groups)
    picked = lax.dynamic_slice_in_dim(grouped, lax.axis_index("gz") * block, block, 2)
    head_block = lax.all_to_all(picked, "gy", split_axis=1, concat_axis=0, tiled=True).reshape(
        seq_dev * row_groups, block
    )
    partial_value = jnp.dot(head_block, out_weight, preferred_element_type=jnp.float32) + jnp.dot(
        hidden, down_weight, preferred_element_type=jnp.float32
    )
    total = lax.psum(partial_value, ("gy", "gz"))
    mixed = (inputs + total).astype(jnp.bfloat16)
    return (mixed, new_kv)


MESH = pl.DeviceIdType.MESH
F32 = jnp.float32
BF16 = jnp.bfloat16


def kernel(
    dims,
    lengths_ref,
    tokens_h,
    gain_h,
    spread_h,
    q_h,
    kv_h,
    cache_h,
    gate_h,
    up_h,
    out_h,
    down_h,
    mixed_ref,
    newkv_ref,
    tokens_v,
    gain_v,
    spread_v,
    q_v,
    kv_v,
    cache_v,
    gate_v,
    up_v,
    out_v,
    down_v,
    load_sem,
    gu_sem,
    down_sem,
    x_v,
    normed_v,
    stat_v,
    qp_v,
    qrs_v,
    kvs_v,
    qsend_v,
    qall_v,
    rot_v,
    newkv_v,
    part_v,
    prs_v,
    side_v,
    srs_v,
    att_v,
    attall_v,
    gsend_v,
    grs_v,
    own_v,
    hid_v,
    acc_v,
    heads_v,
    fin_v,
    stat_sem,
    q_sem,
    kvx_sem,
    qa_sem,
    p_sem,
    s_sem,
    a_sem,
    a_recv,
    g_sem,
    h_sem,
    f_sem,
):
    ngx, ngy, ngz, rows, rp = dims
    gx, gy, gz = lax.axis_index("gx"), lax.axis_index("gy"), lax.axis_index("gz")
    dx = x_v.shape[1]
    qd = q_v.shape[1]
    heads_dev = qd // HEAD_DIM
    own_heads = heads_dev // ngx
    seq_dev = cache_v.shape[0]
    ctx_dev = cache_v.shape[1]
    fb = gate_v.shape[2]
    owners = ngx * ngz
    part_heads = HEADS // owners
    first = gy * seq_dev
    scale = HEAD_DIM ** (-0.5)
    middle = HEAD_DIM // 2

    small = [
        pltpu.make_async_copy(a, b, load_sem.at[i])
        for i, (a, b) in enumerate(
            (
                (tokens_h, tokens_v),
                (gain_h, gain_v),
                (spread_h, spread_v),
                (q_h, q_v),
                (kv_h, kv_v),
                (cache_h, cache_v),
                (out_h, out_v),
            )
        )
    ]

    def gu_copies(step):
        block = lax.rem(gx + 1 + step, ngx)
        columns = pl.ds(pl.multiple_of(block * fb, fb), fb)
        return (
            pltpu.make_async_copy(gate_h.at[:, columns], gate_v.at[step], gu_sem.at[0, step]),
            pltpu.make_async_copy(up_h.at[:, columns], up_v.at[step], gu_sem.at[1, step]),
        )

    def down_copy(step):
        block = lax.rem(gx + step, ngx)
        picked = pl.ds(pl.multiple_of(block * fb, fb), fb)
        return pltpu.make_async_copy(down_h.at[picked], down_v.at[step], down_sem.at[step])

    offsets = [o for o in itertools.product(range(ngx), range(ngy), range(ngz)) if any(o)]

    def shifted(ox, oy, oz):
        return lax.rem(gx + ox, ngx), lax.rem(gy + oy, ngy), lax.rem(gz + oz, ngz)

    def at(px, py, pz):
        return {"gx": px, "gy": py, "gz": pz}

    barrier = pltpu.get_barrier_semaphore()
    for offset in offsets:
        pl.semaphore_signal(barrier, inc=1, device_id=at(*shifted(*offset)), device_id_type=MESH)

    for copy in small[:6]:
        copy.start()
    for copy in gu_copies(0):
        copy.start()

    small[0].wait()
    x_v[...] = jnp.zeros_like(x_v)
    x_v[0:rows, :] = tokens_v[...].astype(F32)
    x = x_v[...]
    lane = lax.broadcasted_iota(jnp.int32, (rp, 128), 1)
    stat_v[gx] = jnp.where(
        lane < 64, jnp.sum(x, 1, keepdims=True), jnp.sum(x * x, 1, keepdims=True)
    )
    small[1].wait()
    spare = lax.broadcasted_iota(jnp.int32, (rp, dx), 0) == rows
    local_mean = stat_v[gx][:, 0:1] / dx
    centred = jnp.where(spare, 1.0, x - local_mean)
    normed_v[...] = (centred * gain_v[...]).astype(BF16)

    qo = own_heads * HEAD_DIM
    small[3].wait()
    for copy in gu_copies(1):
        copy.start()

    @pl.loop(0, ngx)
    def _(j):
        columns = pl.ds(pl.multiple_of(j * qo, qo), qo)
        qp_v[j] = jnp.dot(normed_v[...], q_v[:, columns], preferred_element_type=F32)

    pl.semaphore_wait(barrier, len(offsets))

    pending = []

    def send(source, target, sends, receives, device):
        copy = pltpu.make_async_remote_copy(
            src_ref=source,
            dst_ref=target,
            send_sem=sends,
            recv_sem=receives,
            device_id=device,
            device_id_type=MESH,
        )
        copy.start()
        pending.append(copy)

    def arrived(slot, receives):
        pltpu.make_async_remote_copy(
            src_ref=slot,
            dst_ref=slot,
            send_sem=receives,
            recv_sem=receives,
            device_id=at(gx, gy, gz),
            device_id_type=MESH,
        ).wait_recv()

    for k in range(1, ngx):
        peer = lax.rem(gx + k, ngx)
        send(stat_v.at[gx], stat_v.at[gx], stat_sem.at[0, peer], stat_sem.at[1, gx], at(peer, gy, gz))
        send(qp_v.at[peer], qrs_v.at[gx], q_sem.at[0, peer], q_sem.at[1, gx], at(peer, gy, gz))
    small[4].wait()
    kvs_v[gx] = jnp.dot(normed_v[...], kv_v[...], preferred_element_type=F32)
    for k in range(1, ngx):
        peer = lax.rem(gx + k, ngx)
        send(kvs_v.at[gx], kvs_v.at[gx], kvx_sem.at[0, peer], kvx_sem.at[1, gx], at(peer, gy, gz))
    small[2].wait()

    row = lax.broadcasted_iota(jnp.int32, (rp, middle), 0)
    length = jnp.zeros((rp, middle), jnp.int32)
    for s in range(seq_dev):
        length = jnp.where(row == first + s, lengths_ref[s], length)
    angle = length.astype(F32) * spread_v[...]
    cosine = jnp.cos(angle)
    sine = jnp.sin(angle)

    def moments():
        for k in range(1, ngx):
            peer = lax.rem(gx + k, ngx)
            arrived(stat_v.at[peer], stat_sem.at[1, peer])
        totals = stat_v[0]
        for k in range(1, ngx):
            totals = totals + stat_v[k]
        center = totals[:, 0:1] / D
        spread_sq = totals[:, 64:65] / D - center * center
        return center, lax.rsqrt(spread_sq + epsilon)

    def corrected(part, gain_row, source, center):
        return part + (stat_v[source][:, 0:1] / dx - center) * gain_row

    tile = min(512, fb)

    def gate_up(step):
        for copy in gu_copies(step):
            copy.wait()
        if step + 2 < ngx:
            for copy in gu_copies(step + 2):
                copy.start()
        elif step + 2 == ngx:
            for later in range(ngx):
                down_copy(later).start()
            small[6].start()

        @pl.loop(0, fb // tile)
        def _(n):
            columns = pl.ds(pl.multiple_of(n * tile, tile), tile)
            g = jnp.dot(normed_v[...], gate_v[step, :, columns], preferred_element_type=F32)
            u = jnp.dot(normed_v[...], up_v[step, :, columns], preferred_element_type=F32)
            both = jnp.concatenate([g, u], 0)
            if step < ngx - 1:
                gsend_v[step, :, columns] = both.astype(BF16)
            else:
                own_v[:, columns] = both

        if step < ngx - 1:
            peer = lax.rem(gx + 1 + step, ngx)
            send(gsend_v.at[step], grs_v.at[gx], g_sem.at[0, peer], g_sem.at[1, gx], at(peer, gy, gz))

    def gather_query():
        qrs_v[gx] = qp_v[gx]
        total = None
        for k in range(ngx):
            peer = lax.rem(gx + k, ngx)
            if k:
                arrived(qrs_v.at[peer], q_sem.at[1, peer])
            part = corrected(qrs_v[peer], qrs_v[peer, rows : rows + 1, :], peer, center)
            total = part if total is None else total + part
        total = total * inverse
        mine = (gy * ngz + gz) * heads_dev + gx * own_heads
        for h in range(own_heads):
            piece = total[:, h * HEAD_DIM : (h + 1) * HEAD_DIM].astype(BF16)
            qsend_v[h] = piece
            qall_v[mine + h] = piece
        for offset in offsets:
            px, py, pz = shifted(*offset)
            send(
                qsend_v,
                qall_v.at[pl.ds(mine, own_heads)],
                qa_sem.at[0, px, py, pz],
                qa_sem.at[1, gx, gy, gz],
                at(px, py, pz),
            )

    me_owner = gx * ngz + gz

    def attend():
        keyval = None
        for k in range(ngx):
            peer = lax.rem(gx + k, ngx)
            if k:
                arrived(kvs_v.at[peer], kvx_sem.at[1, peer])
            part = corrected(kvs_v[peer], kvs_v[peer, rows : rows + 1, :], peer, center)
            keyval = part if keyval is None else keyval + part
        keyval = keyval * inverse
        a = keyval[:, :middle]
        b = keyval[:, middle:HEAD_DIM]
        newkv_v[:, :middle] = a * cosine - b * sine
        newkv_v[:, middle:HEAD_DIM] = a * sine + b * cosine
        newkv_v[:, HEAD_DIM:] = keyval[:, HEAD_DIM:]
        picked = newkv_v[0:seq_dev, :]
        for y in range(1, ngy):
            picked = jnp.where(gy == y, newkv_v[y * seq_dev : (y + 1) * seq_dev, :], picked)
        newkv_ref[...] = picked.astype(BF16)
        for offset in offsets:
            px, py, pz = shifted(*offset)
            slot = (py * ngz + pz) * heads_dev + px * own_heads
            arrived(qall_v.at[pl.ds(slot, own_heads)], qa_sem.at[1, px, py, pz])
        q3 = qall_v[...].astype(F32)
        a = q3[:, :, :middle]
        b = q3[:, :, middle:]
        rot_v[:, :, :middle] = (a * cosine - b * sine).astype(BF16).astype(F32)
        rot_v[:, :, middle:] = (a * sine + b * cosine).astype(BF16).astype(F32)
        small[5].wait()
        rotated = rot_v[...].reshape(HEADS * rp, HEAD_DIM).astype(BF16)
        rowid = lax.rem(lax.broadcasted_iota(jnp.int32, (HEADS * rp, ctx_dev), 0), rp)
        position = (gx * ngz + gz) * ctx_dev + lax.broadcasted_iota(
            jnp.int32, (HEADS * rp, ctx_dev), 1
        )
        scores = jnp.full((HEADS * rp, ctx_dev), masked_fill, F32)
        limit = jnp.zeros((HEADS * rp, ctx_dev), jnp.int32)
        for s in range(seq_dev):
            raw = lax.dot_general(
                rotated,
                cache_v[s, :, :HEAD_DIM],
                (((1,), (1,)), ((), ())),
                preferred_element_type=F32,
            )
            limit = jnp.where(rowid == first + s, lengths_ref[s], limit)
            scores = jnp.where(rowid == first + s, raw * scale, scores)
        live = position < limit
        scores = jnp.where(live, scores, masked_fill)
        top = jnp.max(scores, 1, keepdims=True)
        weights = jnp.where(live, jnp.exp(scores - top), 0.0)
        denom = jnp.sum(weights, 1, keepdims=True)
        numer = jnp.zeros((HEADS * rp, HEAD_DIM), F32)
        for s in range(seq_dev):
            numer = numer + jnp.dot(
                jnp.where(rowid == first + s, weights, 0.0).astype(BF16),
                cache_v[s, :, HEAD_DIM:],
                preferred_element_type=F32,
            )
        part_v[...] = numer.reshape(HEADS, rp, HEAD_DIM).astype(BF16)
        wide = 64 // part_heads
        lanes = lax.broadcasted_iota(jnp.int32, (owners, rp, 128), 2)
        top4 = jnp.broadcast_to(top, (HEADS * rp, 128)).reshape(owners, part_heads, rp, 128)
        denom4 = jnp.broadcast_to(denom, (HEADS * rp, 128)).reshape(owners, part_heads, rp, 128)
        packed = jnp.zeros((owners, rp, 128), F32)
        for h in range(part_heads):
            low = lanes >= h * wide
            packed = jnp.where(low & (lanes < 64), top4[:, h], packed)
            packed = jnp.where(lanes >= 64 + h * wide, denom4[:, h], packed)
        side_v[...] = packed
        for ox, oz in itertools.product(range(ngx), range(ngz)):
            if ox or oz:
                px, py, pz = shifted(ox, 0, oz)
                peer = px * ngz + pz
                send(
                    part_v.at[pl.ds(peer * part_heads, part_heads)],
                    prs_v.at[me_owner],
                    p_sem.at[0, peer],
                    p_sem.at[1, me_owner],
                    at(px, py, pz),
                )
                send(
                    side_v.at[peer],
                    srs_v.at[me_owner],
                    s_sem.at[0, peer],
                    s_sem.at[1, me_owner],
                    at(px, py, pz),
                )

    block = (me_owner * part_heads) // heads_dev
    by, bz = block // ngz, lax.rem(block, ngz)
    local = lax.rem(me_owner, heads_dev // part_heads)

    def combine_parts():
        prs_v[me_owner] = part_v[pl.ds(me_owner * part_heads, part_heads)]
        srs_v[me_owner] = side_v[me_owner]
        for ox, oz in itertools.product(range(ngx), range(ngz)):
            if ox or oz:
                px, py, pz = shifted(ox, 0, oz)
                peer = px * ngz + pz
                arrived(prs_v.at[peer], p_sem.at[1, peer])
                arrived(srs_v.at[peer], s_sem.at[1, peer])
        wide = 64 // part_heads

        def column(o, start):
            return jnp.stack(
                [
                    srs_v[o, :, start + h * wide : start + h * wide + 1]
                    for h in range(part_heads)
                ]
            )

        rot = rot_v[pl.ds(me_owner * part_heads, part_heads)]
        newkv = newkv_v[...].astype(BF16).astype(F32)
        own = jnp.sum(rot * newkv[:, :HEAD_DIM], 2, keepdims=True) * scale
        tops = [column(o, 0) for o in range(owners)]
        top = own
        for t in tops:
            top = jnp.maximum(top, t)
        weight = jnp.exp(own - top)
        numer = weight * newkv[:, HEAD_DIM:]
        denom = weight
        for o in range(owners):
            factor = jnp.exp(tops[o] - top)
            numer = numer + factor * prs_v[o].astype(F32)
            denom = denom + factor * column(o, 64)
        rowid = lax.broadcasted_iota(jnp.int32, (part_heads, rp, HEAD_DIM), 1)
        mine = (rowid >= first) & (rowid < first + seq_dev)
        att_v[...] = jnp.where(mine, numer / denom, 0.0).astype(BF16)
        for k in range(ngx):
            px = lax.rem(gx + k, ngx)
            copy = pltpu.make_async_remote_copy(
                src_ref=att_v,
                dst_ref=attall_v.at[gy, local],
                send_sem=a_sem.at[px],
                recv_sem=a_recv.at[gy, local],
                device_id=at(px, by, bz),
                device_id_type=MESH,
            )
            if k:
                copy.start()
                pending.append(copy)
            else:
                same = (by == gy) & (bz == gz)

                @pl.when(same)
                def _():
                    attall_v[gy, local] = att_v[...]

                @pl.when(jnp.logical_not(same))
                def _(copy=copy):
                    copy.start()
                    copy.wait_send()

    def gather_heads():
        for sy in range(ngy):
            for sl in range(heads_dev // part_heads):
                owner = (gy * ngz + gz) * (heads_dev // part_heads) + sl
                theirs = (sy == gy) & (owner == me_owner)

                @pl.when(jnp.logical_not(theirs))
                def _(sy=sy, sl=sl):
                    arrived(attall_v.at[sy, sl], a_recv.at[sy, sl])

        pieces = []
        for h in range(heads_dev):
            total = attall_v[0, h // part_heads, h % part_heads].astype(F32)
            for sy in range(1, ngy):
                total = total + attall_v[sy, h // part_heads, h % part_heads].astype(F32)
            pieces.append(total.astype(BF16))
        mixed_heads = jnp.concatenate(pieces, 1)
        small[6].wait()
        heads_v[...] = mixed_heads

    def out_product(low, high):
        @pl.loop(low // ct, high // ct)
        def _(n):
            columns = pl.ds(pl.multiple_of(n * ct, ct), ct)
            acc_v[:, columns] += jnp.dot(
                heads_v[...], out_v[:, columns], preferred_element_type=F32
            )

    gate_up(0)
    center, inverse = moments()
    gather_query()
    for step in range(1, ngx - 1):
        gate_up(step)
    attend()
    gate_up(ngx - 1)

    g = u = None
    for k in range(ngx):
        peer = lax.rem(gx + k, ngx)
        if k:
            arrived(grs_v.at[peer], g_sem.at[1, peer])
            both = grs_v[peer].astype(F32)
        else:
            both = own_v[...]
        g_part = corrected(both[:rp], both[rows : rows + 1], peer, center)
        u_part = corrected(both[rp:], both[rp + rows : rp + rows + 1], peer, center)
        g = g_part if g is None else g + g_part
        u = u_part if u is None else u + u_part
    g = g * inverse
    u = u * inverse
    hid_v[gx] = (g / (1.0 + jnp.exp(-g)) * u).astype(BF16)
    for k in range(1, ngx):
        peer = lax.rem(gx + k, ngx)
        send(hid_v.at[gx], hid_v.at[gx], h_sem.at[0, peer], h_sem.at[1, gx], at(peer, gy, gz))

    combine_parts()
    spot = gy * ngz + gz
    ct = min(512, dx // 2)
    half = dx // 2
    peers = [o for o in itertools.product(range(ngy), range(ngz)) if any(o)]

    def down_product(step, low, high):
        source = lax.rem(gx + step, ngx)

        @pl.loop(low // ct, high // ct)
        def _(n):
            columns = pl.ds(pl.multiple_of(n * ct, ct), ct)
            product = jnp.dot(
                hid_v[source], down_v[step, :, columns], preferred_element_type=F32
            )
            if step:
                acc_v[:, columns] += product
            else:
                acc_v[:, columns] = product

    for step in range(ngx):
        source = lax.rem(gx + step, ngx)
        down_copy(step).wait()
        if step:
            arrived(hid_v.at[source], h_sem.at[1, source])
        down_product(step, 0, dx)
    gather_heads()
    for part in range(2):
        out_product(part * half, (part + 1) * half)
        fin_v[part, spot] = acc_v[:, part * half : (part + 1) * half].astype(BF16)
        for oy, oz in peers:
            px, py, pz = shifted(0, oy, oz)
            peer = py * ngz + pz
            send(
                fin_v.at[part, spot],
                fin_v.at[part, spot],
                f_sem.at[0, part, peer],
                f_sem.at[1, part, spot],
                at(px, py, pz),
            )
    for part in range(2):
        columns = slice(part * half, (part + 1) * half)
        total = x_v[:, columns] + acc_v[:, columns]
        for oy, oz in peers:
            px, py, pz = shifted(0, oy, oz)
            peer = py * ngz + pz
            arrived(fin_v.at[part, peer], f_sem.at[1, part, peer])
            total = total + fin_v[part, peer].astype(F32)
        mixed_ref[:, columns] = total[:rows].astype(BF16)
    for copy in pending:
        copy.wait_send()


def fused(sizes, *args):
    (tokens, gain, qw, kvw, outw, gatew, upw, downw, cache, lengths) = args
    ngx, ngy, ngz = sizes
    rows, dx = tokens.shape
    rp = (rows // 8 + 1) * 8
    qd = qw.shape[1]
    fb = gatew.shape[1] // ngx
    own_heads = qd // HEAD_DIM // ngx
    heads_dev = qd // HEAD_DIM
    owners = ngx * ngz
    part_heads = HEADS // owners
    middle = HEAD_DIM // 2
    spread = np.power(
        np.float32(rotary_base), -np.arange(middle, dtype=np.float32) / np.float32(middle)
    ).reshape(1, middle)
    dma = pltpu.SemaphoreType.DMA
    vm = pltpu.VMEM
    scratch = [
        vm(tokens.shape, BF16),
        vm((1, dx), F32),
        vm((1, middle), F32),
        vm(qw.shape, BF16),
        vm(kvw.shape, BF16),
        vm(cache.shape, BF16),
        vm((ngx, dx, fb), BF16),
        vm((ngx, dx, fb), BF16),
        vm(outw.shape, BF16),
        vm((ngx, fb, dx), BF16),
        dma((7,)),
        dma((2, ngx)),
        dma((ngx,)),
        vm((rp, dx), F32),
        vm((rp, dx), BF16),
        vm((ngx, rp, 128), F32),
        vm((ngx, rp, own_heads * HEAD_DIM), F32),
        vm((ngx, rp, own_heads * HEAD_DIM), F32),
        vm((ngx, rp, 2 * HEAD_DIM), F32),
        vm((own_heads, rp, HEAD_DIM), BF16),
        vm((HEADS, rp, HEAD_DIM), BF16),
        vm((HEADS, rp, HEAD_DIM), F32),
        vm((rp, 2 * HEAD_DIM), F32),
        vm((HEADS, rp, HEAD_DIM), BF16),
        vm((owners, part_heads, rp, HEAD_DIM), BF16),
        vm((owners, rp, 128), F32),
        vm((owners, rp, 128), F32),
        vm((part_heads, rp, HEAD_DIM), BF16),
        vm((ngy, heads_dev // part_heads, part_heads, rp, HEAD_DIM), BF16),
        vm((ngx - 1, 2 * rp, fb), BF16),
        vm((ngx, 2 * rp, fb), BF16),
        vm((2 * rp, fb), F32),
        vm((ngx, rp, fb), BF16),
        vm((rp, dx), F32),
        vm((rp, qd), BF16),
        vm((2, ngy * ngz, rp, dx // 2), BF16),
        dma((2, ngx)),
        dma((2, ngx)),
        dma((2, ngx)),
        dma((2, ngx, ngy, ngz)),
        dma((2, owners)),
        dma((2, owners)),
        dma((ngx,)),
        dma((ngy, heads_dev // part_heads)),
        dma((2, ngx)),
        dma((2, ngx)),
        dma((2, 2, ngy * ngz)),
    ]
    anywhere = pl.BlockSpec(memory_space=pl.ANY)
    return pl.pallas_call(
        functools.partial(kernel, (ngx, ngy, ngz, rows, rp)),
        out_shape=(
            pltpu.VMEM(tokens.shape, BF16),
            pltpu.VMEM((cache.shape[0], 2 * HEAD_DIM), BF16),
        ),
        in_specs=[pl.BlockSpec(memory_space=pltpu.SMEM)] + [anywhere] * 10,
        out_specs=(pl.BlockSpec(memory_space=pltpu.VMEM),) * 2,
        scratch_shapes=scratch,
        compiler_params=pltpu.CompilerParams(
            collective_id=0, has_side_effects=True, vmem_limit_bytes=61 * 2**20
        ),
    )(lengths, tokens, gain.reshape(1, dx), spread, qw, kvw, cache, gatew, upw, outw, downw)


def fits(sizes, d_dev, q_dev, ff_dev, weight_bytes):
    ngx, ngy, ngz = sizes
    heads_dev = q_dev // HEAD_DIM
    return (
        ngx >= 3
        and HEADS // (ngx * ngz) in (1, 2, 4)
        and d_dev % 1024 == 0
        and heads_dev % ngx == 0
        and HEADS % (ngx * ngz) == 0
        and heads_dev % (HEADS // (ngx * ngz)) == 0
        and ff_dev % (ngx * 128) == 0
        and weight_bytes <= 60 * 2**20
    )


def choose(sizes, *args):
    held = sum(a.size * a.dtype.itemsize for a in args[2:9])
    if fits(sizes, args[0].shape[1], args[2].shape[1], args[5].shape[1], held):
        return fused(sizes, *args)
    return body(*args)


def solution(mesh):
    sizes = tuple(mesh.shape[a] for a in ("gx", "gy", "gz"))
    chosen = functools.partial(choose, sizes)
    in_specs = (
        P("group", "gx"),
        P("gx"),
        P("gx", ("gy", "gz")),
        P("gx", None),
        P(("gy", "gz"), "gx"),
        P("gx", ("gy", "gz")),
        P("gx", ("gy", "gz")),
        P(("gy", "gz"), "gx"),
        P(("group", "gy"), ("gx", "gz"), None),
        P(("group", "gy")),
    )
    out_specs = (P("group", "gx"), P(("group", "gy"), None))
    return jax.shard_map(chosen, mesh=mesh, in_specs=in_specs, out_specs=out_specs, check_vma=False)
```
